32 devices in a mesh: seq: 16 (over z, x, core), tp: 2 (over y).
Axes of the slice: x: 2, y: 2, z: 4, core: 2. Of those that a mesh axis runs over, the one named last changes fastest.
Arguments:
- tokens: bfloat16 [2048, 5120], P('seq', 'tp'), may hold values from -4 to 4
- self_queries: bfloat16 [2048, 3072], P('seq', 'tp'), may hold values from -12 to 12
- self_keys: bfloat16 [2048, 3072], P('seq', 'tp'), may hold values from -12 to 12
- self_values: bfloat16 [2048, 3072], P('seq', 'tp'), may hold values from -6 to 6
- cross_queries: bfloat16 [2048, 3072], P('seq', 'tp'), may hold values from -12 to 12
- caption_keys: bfloat16 [512, 3072], P('seq', 'tp'), may hold values from -12 to 12
- caption_values: bfloat16 [512, 3072], P('seq', 'tp'), may hold values from -6 to 6
- out_weight: bfloat16 [3072, 5120], P('tp'), may hold values from -0.15625 to 0.15625
- gate_vector: float32 [5120], P('tp'), may hold values from -6 to 6
Outputs:
- updated: bfloat16 [2048, 5120], P('seq', 'tp')
- cross_heads: bfloat16 [2048, 3072], P('seq', 'tp')
The draws below stay inside these ranges and needn't reach their ends.
All inputs are finite; a program needn't handle non-finite values.
Results may differ from the reference program's by a relative error of at most 0.0085.
Values may be sent and summed in bfloat16 or wider, within the bound.
No kernel may reach another device: no remote copies, remote signals or barrier semaphores. Data moves between devices by JAX's collectives and lax.ppermute only.
A program may use at most 128 MiB of HBM per device.

```python
import math
import jax
import jax.numpy as jnp
from jax import lax

D = 5120
HEADS = 24
DH = 128
CAP = 512
TOK_DEV = 128
TOKENS = 2048


def draw_pair(key, query_rows, key_rows, salt):
    width = HEADS * DH
    base = jax.random.fold_in(key, salt)
    queries = jnp.clip(1.4 * jax.random.normal(jax.random.fold_in(base, 1), (query_rows, width), jnp.float32), -8.4, 8.4)
    keys_drawn = jnp.clip(1.4 * jax.random.normal(jax.random.fold_in(base, 2), (key_rows, width), jnp.float32), -8.4, 8.4)
    return (queries, keys_drawn)


def draw_self_queries(key, part):
    return draw_pair(key, TOKENS, TOKENS, 7)[0].astype(jnp.bfloat16)


def draw_self_keys(key, part):
    return draw_pair(key, TOKENS, TOKENS, 7)[1].astype(jnp.bfloat16)


def draw_cross_queries(key, part):
    return draw_pair(key, TOKENS, CAP, 9)[0].astype(jnp.bfloat16)


def draw_caption_keys(key, part):
    return draw_pair(key, TOKENS, CAP, 9)[1].astype(jnp.bfloat16)


def with_spikes(values, stream_key, source, target, shards_of, factor):
    owner, partner = [(jnp.arange(values.shape[position]) // (values.shape[position] // shards_of)).reshape([-1 if axis == position else 1 for axis in range(values.ndim)]) for position in (source, target)]
    chosen = jax.random.permutation(stream_key, shards_of)[partner]
    strong = (owner == chosen) | (owner == (partner + shards_of // 2) % shards_of)
    return jnp.where(strong, factor * values, values)


def steps_of(key, shape, shards, smallest, high):
    loudness, own = 1.0, jax.random.fold_in(key, 6)
    for axis_at, shards_of in shards:
        heights = jnp.exp(jax.random.uniform(jax.random.fold_in(own, axis_at), (shards_of,), jnp.float32, smallest / len(shards), high / len(shards)))
        loudness = loudness * jnp.repeat(heights, shape[axis_at] // shards_of).reshape([-1 if axis == axis_at else 1 for axis in range(len(shape))])
    return loudness


def gaussian(key, extent, scale, most, split=(), held_as=jnp.bfloat16):
    entries = scale * jax.random.normal(key, extent, jnp.float32)
    if split:
        entries = entries * steps_of(key, extent, split, -0.22, 0.18)
    return jnp.clip(entries, -most, most).astype(held_as)


def heavy_noise(own_key, extent, deviation, reach, pieces, heavy, held_as=jnp.bfloat16):
    array = deviation * jax.random.normal(own_key, extent, jnp.float32)
    if pieces:
        array = array * steps_of(own_key, extent, pieces, -0.22, 0.18)
    return jnp.clip(with_spikes(array, jax.random.fold_in(own_key, 3), *heavy), -reach, reach).astype(held_as)


def setup_inputs(seed: int = 0) -> dict:
    arg_keys = jax.random.split(jax.random.key(seed), 10)
    tokens = gaussian(arg_keys[0], (TOKENS, D), 0.5, 4.0, ((0, 16), (1, 2)))
    self_queries = draw_self_queries(jax.random.fold_in(arg_keys[9], 71), 0)
    self_keys = draw_self_keys(jax.random.fold_in(arg_keys[9], 71), 0)
    self_values = gaussian(arg_keys[3], (TOKENS, HEADS * DH), 1.0, 6.0, ((0, 16), (1, 2)))
    cross_queries = draw_cross_queries(jax.random.fold_in(arg_keys[9], 71), 0)
    caption_keys = draw_caption_keys(jax.random.fold_in(arg_keys[9], 71), 0)
    caption_values = gaussian(arg_keys[6], (CAP, HEADS * DH), 1.0, 6.0, ((0, 16), (1, 2)))
    out_weight = heavy_noise(arg_keys[7], (HEADS * DH, D), (HEADS * DH) ** -0.5, 0.15625, ((0, 2),), (0, 1, 2, 2.0))
    gate_vector = gaussian(arg_keys[8], (D,), 1.5, 6.0, ((0, 2),), jnp.float32)
    return {"tokens": tokens, "self_queries": self_queries, "self_keys": self_keys, "self_values": self_values, "cross_queries": cross_queries, "caption_keys": caption_keys, "caption_values": caption_values, "out_weight": out_weight, "gate_vector": gate_vector}


def attend(queries, keys_all, values_all):
    row_total = queries.shape[0]
    key_total = keys_all.shape[0]
    score_scale = 1.0 / math.sqrt(DH)
    keys_split = keys_all.astype(jnp.float32).reshape(key_total, HEADS, DH)
    values_split = values_all.astype(jnp.float32).reshape(key_total, HEADS, DH)
    blocks = queries.reshape(row_total // TOK_DEV, TOK_DEV, HEADS, DH)

    def one_block(query_block):
        scores = jnp.einsum('thd,khd->thk', query_block.astype(jnp.float32), keys_split) * score_scale
        maxima = lax.optimization_barrier(jnp.max(scores, axis=2))
        exp_scores = jnp.exp(scores - maxima[:, :, None])
        totals = lax.optimization_barrier(jnp.sum(exp_scores, axis=2))
        weights = lax.optimization_barrier(exp_scores.astype(jnp.bfloat16)).astype(jnp.float32)
        mixed = jnp.einsum('thk,khd->thd', weights, values_split)
        return (mixed / totals[:, :, None]).reshape(TOK_DEV, HEADS * DH).astype(jnp.bfloat16)
    return lax.map(one_block, blocks).reshape(row_total, HEADS * DH)

def reference(tokens, self_queries, self_keys, self_values, cross_queries, caption_keys, caption_values, out_weight, gate_vector):
    self_heads = attend(self_queries, self_keys, self_values)
    cross_heads = attend(cross_queries, caption_keys, caption_values)
    projected = jnp.dot(self_heads, out_weight, preferred_element_type=jnp.float32)
    updated = (tokens.astype(jnp.float32) + gate_vector[None, :] * projected).astype(jnp.bfloat16)
    return (updated, cross_heads)
```

```python
import math

import jax
import jax.numpy as jnp
from jax import lax
from jax.experimental import pallas as pl
from jax.experimental.pallas import tpu as pltpu
from jax.sharding import PartitionSpec as P

DH = 128
F32 = jnp.float32
BF16 = jnp.bfloat16
VMEM = pltpu.VMEM
LOG2E = 1.4426950408889634


def whole():
    return pl.BlockSpec(memory_space=VMEM)


def cost(flops, nbytes, transcendentals=0):
    return pl.CostEstimate(
        flops=int(flops), bytes_accessed=int(nbytes), transcendentals=int(transcendentals)
    )


def softmax_mix(query, keys, values, factor):
    scores = [
        lax.dot_general(query, block, (((1,), (1,)), ((), ())), preferred_element_type=F32)
        for block in keys
    ]
    top = jnp.max(scores[0], axis=1, keepdims=True)
    for block in scores[1:]:
        top = jnp.maximum(top, jnp.max(block, axis=1, keepdims=True))
    total = None
    mixed = None
    for block, value in zip(scores, values):
        weight = jnp.exp2((block - top) * factor)
        part = jnp.sum(weight, axis=1, keepdims=True)
        total = part if total is None else total + part
        term = jnp.dot(weight.astype(BF16), value, preferred_element_type=F32)
        mixed = term if mixed is None else mixed + term
    return mixed / total


def pack_kernel(groups, zi_ref, q_ref, k_ref, v_ref, ck_ref, cv_ref, *outs):
    width = q_ref.shape[1] // groups
    heads = width // DH
    zi = zi_ref[0]
    for r in range(groups):
        base = pl.multiple_of(lax.rem(zi + r, groups) * width, DH)
        outs[r][...] = q_ref[:, pl.ds(base, width)]
        for h in range(heads):
            out = outs[groups + r * heads + h]
            at = pl.multiple_of(base + h * DH, DH)
            out[:, :DH] = k_ref[:, pl.ds(at, DH)]
            out[:, DH:] = v_ref[:, pl.ds(at, DH)]
    cap = outs[-1]
    rows = ck_ref.shape[0]
    cap[:rows, :] = ck_ref[...]
    cap[rows:, :] = cv_ref[...]


def pack(groups, zi, q, k, v, ck, cv):
    rows, columns = q.shape
    width = columns // groups
    heads = width // DH
    shapes = [jax.ShapeDtypeStruct((rows, width), BF16)] * groups
    shapes += [jax.ShapeDtypeStruct((rows, 2 * DH), BF16)] * (groups * heads)
    shapes += [jax.ShapeDtypeStruct((2 * ck.shape[0], columns), BF16)]
    outs = pl.pallas_call(
        lambda *refs: pack_kernel(groups, *refs),
        out_shape=shapes,
        in_specs=[pl.BlockSpec(memory_space=pltpu.SMEM)] + [whole()] * 5,
        out_specs=[whole()] * len(shapes),
        cost_estimate=cost(0, 6 * rows * columns * 2),
        name="pack",
    )(zi, q, k, v, ck, cv)
    queries = outs[:groups]
    pairs = [outs[groups + r * heads : groups + (r + 1) * heads] for r in range(groups)]
    return queries, pairs, outs[-1]


def attend_kernel(parts, head, factor, *refs):
    queries, pairs, outs = refs[:parts], refs[parts:-parts], refs[-parts:]
    keys = [ref[:, :DH] for ref in pairs]
    values = [ref[:, DH:] for ref in pairs]
    for query, out in zip(queries, outs):
        out[...] = softmax_mix(
            query[:, head * DH : (head + 1) * DH], keys, values, factor
        ).astype(BF16)


def attend(queries, pairs, head, factor):
    parts = len(queries)
    rows = queries[0].shape[0]
    total_keys = sum(p.shape[0] for p in pairs)
    return pl.pallas_call(
        lambda *refs: attend_kernel(parts, head, factor, *refs),
        out_shape=[jax.ShapeDtypeStruct((rows, DH), BF16)] * parts,
        in_specs=[whole()] * (parts + len(pairs)),
        out_specs=[whole()] * parts,
        cost_estimate=cost(
            4 * parts * rows * total_keys * DH, total_keys * DH * 4, parts * rows * total_keys
        ),
        name="attend_%d" % head,
    )(*queries, *pairs)


def cross_kernel(factor, q_ref, *refs):
    pieces, out = refs[:-1], refs[-1]
    rows = pieces[0].shape[0] // 2
    for h in range(q_ref.shape[1] // DH):
        at = slice(h * DH, (h + 1) * DH)
        keys = jnp.concatenate([p[:rows, at] for p in pieces], axis=0)
        values = jnp.concatenate([p[rows:, at] for p in pieces], axis=0)
        out[:, at] = softmax_mix(q_ref[:, at], [keys], [values], factor).astype(BF16)


def cross(q, pieces, factor):
    rows, columns = q.shape
    total_keys = sum(p.shape[0] for p in pieces) // 2
    return pl.pallas_call(
        lambda *refs: cross_kernel(factor, *refs),
        out_shape=jax.ShapeDtypeStruct((rows, columns), BF16),
        in_specs=[whole()] * (1 + len(pieces)),
        out_specs=whole(),
        cost_estimate=cost(
            4 * rows * total_keys * columns,
            (2 * rows + 2 * total_keys) * columns * 2,
            rows * total_keys * columns // DH,
        ),
        name="cross",
    )(q, *pieces)


def project_kernel(groups, heads, at_ref, *refs):
    lhs, w_ref, out = refs[: groups * heads], refs[-2], refs[-1]
    width = heads * DH
    total = None
    for r in range(groups):
        base = pl.multiple_of(lax.rem(at_ref[0] + r, groups) * width, DH)
        left = jnp.concatenate([lhs[r * heads + h][...] for h in range(heads)], axis=1)
        term = jnp.dot(left, w_ref[pl.ds(base, width), :], preferred_element_type=F32)
        total = term if total is None else total + term
    out[...] = total.astype(out.dtype)


def project(groups, at, lhs, weight, columns, dtype, name):
    heads = len(lhs) // groups
    rows = lhs[0].shape[0]
    depth = weight.shape[0]
    block = math.gcd(columns, 512)
    steps = columns // block
    return pl.pallas_call(
        lambda *refs: project_kernel(groups, heads, *refs),
        out_shape=jax.ShapeDtypeStruct((rows, columns), dtype),
        grid_spec=pltpu.PrefetchScalarGridSpec(
            num_scalar_prefetch=1,
            grid=(steps,),
            in_specs=[pl.BlockSpec((rows, DH), lambda n, at: (0, 0))] * len(lhs)
            + [pl.BlockSpec((depth, block), lambda n, at: (0, at[1] * steps + n))],
            out_specs=pl.BlockSpec((rows, block), lambda n, at: (0, n)),
        ),
        cost_estimate=cost(
            2 * rows * depth * columns, depth * columns * 2 + rows * columns * 4
        ),
        name=name,
    )(at, *lhs, weight)


def shards(
    seq_size,
    tp_size,
    tokens,
    self_queries,
    self_keys,
    self_values,
    cross_queries,
    caption_keys,
    caption_values,
    out_weight,
    gate_vector,
):
    rows, columns = self_queries.shape
    heads_here = columns // DH
    factor = LOG2E / math.sqrt(DH)
    groups = math.gcd(heads_here, seq_size)
    members = seq_size // groups
    heads = heads_here // groups
    zi = (lax.axis_index("seq") // members).astype(jnp.int32)
    tpi = lax.axis_index("tp").astype(jnp.int32)

    def rotate(x, r):
        if r % groups == 0:
            return x
        step = (r % groups) * members
        return lax.ppermute(x, "seq", [(s, (s + step) % seq_size) for s in range(seq_size)])

    def swap(x, bit):
        return lax.ppermute(x, "seq", [(s, s ^ bit) for s in range(seq_size)])

    def spread(pieces):
        if members & (members - 1):
            index_groups = [
                [g * members + m for m in range(members)] for g in range(groups)
            ]
            return [
                part
                for x in pieces
                for part in lax.all_gather(x, "seq", axis=0, axis_index_groups=index_groups)
            ]
        bit = members // 2
        while bit:
            pieces = pieces + [swap(x, bit) for x in pieces]
            bit //= 2
        return pieces

    queries, pairs, caption = pack(
        groups, zi[None], self_queries, self_keys, self_values, caption_keys, caption_values
    )
    queries = [rotate(x, r) for r, x in enumerate(queries)]
    mixed = []
    for h in range(heads):
        mine = jnp.concatenate([rotate(pairs[r][h], r) for r in range(groups)], axis=0)
        outs = attend(queries, spread([mine]), h, factor)
        mixed.append([rotate(x, groups - r) for r, x in enumerate(outs)])

    captions = jnp.concatenate([rotate(caption, r) for r in range(groups)], axis=0)
    captions = spread([captions])
    cap_rows = caption.shape[0]
    pieces = [x[g * cap_rows : (g + 1) * cap_rows] for x in captions for g in range(groups)]
    cross_heads = cross(cross_queries, pieces, factor)

    lhs = [mixed[h][r] for r in range(groups) for h in range(heads)]
    out_columns = tokens.shape[1]
    if tp_size == 2:
        away = project(
            groups, jnp.stack([zi, 1 - tpi]), lhs, out_weight, out_columns, BF16, "away"
        )
        away = lax.ppermute(away, "tp", [(0, 1), (1, 0)])
        home = project(groups, jnp.stack([zi, tpi]), lhs, out_weight, out_columns, F32, "home")
        projected = home + away.astype(F32)
    else:
        both = project(
            groups,
            jnp.stack([zi, jnp.zeros_like(tpi)]),
            lhs,
            out_weight,
            out_weight.shape[1],
            BF16,
            "home",
        )
        projected = lax.psum_scatter(both, "tp", scatter_dimension=1, tiled=True).astype(F32)
    updated = (tokens.astype(F32) + gate_vector[None, :] * projected).astype(BF16)
    return (updated, cross_heads)


def solution(mesh):
    seq_size, tp_size = mesh.shape["seq"], mesh.shape["tp"]
    return jax.shard_map(
        lambda *args: shards(seq_size, tp_size, *args),
        mesh=mesh,
        in_specs=(
            P("seq", "tp"),
            P("seq", "tp"),
            P("seq", "tp"),
            P("seq", "tp"),
            P("seq", "tp"),
            P("seq", "tp"),
            P("seq", "tp"),
            P("tp", None),
            P("tp"),
        ),
        out_specs=(P("seq", "tp"), P("seq", "tp")),
        check_vma=False,
    )
```

```python
import math

import jax
import jax.numpy as jnp
from jax import lax
from jax.experimental import pallas as pl
from jax.experimental.pallas import tpu as pltpu
from jax.sharding import PartitionSpec as P

DH = 128
F32 = jnp.float32
BF16 = jnp.bfloat16
LOG2E = 1.4426950408889634


def in_vmem():
    return pl.BlockSpec(memory_space=pltpu.VMEM)


def in_smem():
    return pl.BlockSpec(memory_space=pltpu.SMEM)


def cost(flops, nbytes, transcendentals=0):
    return pl.CostEstimate(
        flops=int(flops), bytes_accessed=int(nbytes), transcendentals=int(transcendentals)
    )


def shape(rows, columns, dtype=BF16):
    return jax.ShapeDtypeStruct((rows, columns), dtype)


def after(x, *others):
    return lax.optimization_barrier((x, others))[0]


def softmax_mix(query, keys, values, factor):
    scores = [
        lax.dot_general(query, block, (((1,), (1,)), ((), ())), preferred_element_type=F32)
        for block in keys
    ]
    top = jnp.max(scores[0], axis=1, keepdims=True)
    for block in scores[1:]:
        top = jnp.maximum(top, jnp.max(block, axis=1, keepdims=True))
    total = None
    mixed = None
    for block, value in zip(scores, values):
        weight = jnp.exp2((block - top) * factor)
        part = jnp.sum(weight, axis=1, keepdims=True)
        total = part if total is None else total + part
        term = jnp.dot(weight.astype(BF16), value, preferred_element_type=F32)
        mixed = term if mixed is None else mixed + term
    return mixed / total


def pack_kernel(groups, at_ref, q_ref, k_ref, v_ref, *outs):
    width = q_ref.shape[1] // groups
    heads = width // DH
    for r in range(groups):
        base = lax.rem(at_ref[0] + r, groups) * width
        for h in range(heads):
            at = pl.ds(pl.multiple_of(base + h * DH, DH), DH)
            out = outs[r * heads + h]
            out[:, :DH] = q_ref[:, at]
            out[:, DH : 2 * DH] = k_ref[:, at]
            out[:, 2 * DH :] = v_ref[:, at]


def pack(groups, at, q, k, v):
    rows, columns = q.shape
    heads = columns // groups // DH
    outs = pl.pallas_call(
        lambda *refs: pack_kernel(groups, *refs),
        out_shape=[shape(rows, 3 * DH)] * (groups * heads),
        in_specs=[in_smem()] + [in_vmem()] * 3,
        out_specs=[in_vmem()] * (groups * heads),
        cost_estimate=cost(0, 6 * rows * columns * 2),
        name="pack",
    )(at, q, k, v)
    return [outs[r * heads : (r + 1) * heads] for r in range(groups)]


def pack_cross_kernel(at_ref, q_ref, k_ref, v_ref, *outs):
    half = q_ref.shape[1] // 2
    rows = k_ref.shape[0]
    for i in range(2):
        side = at_ref[1] if i == 0 else 1 - at_ref[1]
        at = pl.ds(pl.multiple_of(side * half, DH), half)
        outs[i][...] = q_ref[:, at]
        outs[2 + i][:rows, :] = k_ref[:, at]
        outs[2 + i][rows:, :] = v_ref[:, at]


def pack_cross(at, q, k, v):
    rows, columns = q.shape
    return pl.pallas_call(
        pack_cross_kernel,
        out_shape=[shape(rows, columns // 2)] * 2 + [shape(2 * k.shape[0], columns // 2)] * 2,
        in_specs=[in_smem()] + [in_vmem()] * 3,
        out_specs=[in_vmem()] * 4,
        cost_estimate=cost(0, 4 * (rows + 2 * k.shape[0]) * columns),
        name="pack_cross",
    )(at, q, k, v)


def attend_kernel(parts, factor, *refs):
    queries, pairs, outs = refs[:parts], refs[parts:-parts], refs[-parts:]
    keys = [ref[:, :DH] for ref in pairs]
    values = [ref[:, DH:] for ref in pairs]
    for query, out in zip(queries, outs):
        out[...] = softmax_mix(query[:, :DH], keys, values, factor).astype(BF16)


def attend(queries, pairs, factor, name):
    parts = len(queries)
    rows = queries[0].shape[0]
    total_keys = sum(p.shape[0] for p in pairs)
    return pl.pallas_call(
        lambda *refs: attend_kernel(parts, factor, *refs),
        out_shape=[shape(rows, DH)] * parts,
        in_specs=[in_vmem()] * (parts + len(pairs)),
        out_specs=[in_vmem()] * parts,
        cost_estimate=cost(
            4 * parts * rows * total_keys * DH, total_keys * DH * 4, parts * rows * total_keys
        ),
        name=name,
    )(*queries, *pairs)


def cross_kernel(factor, block, parts, *refs):
    queries, captions, outs = refs[:parts], refs[parts:-parts], refs[-parts:]
    for h in range(queries[0].shape[1] // DH):
        at = slice(h * DH, (h + 1) * DH)
        keys, values = [
            jnp.concatenate(
                [
                    c[b * block : (b + 1) * block, at]
                    for c in captions
                    for b in range(first, c.shape[0] // block, 2)
                ],
                axis=0,
            )
            for first in (0, 1)
        ]
        for query, out in zip(queries, outs):
            out[:, at] = softmax_mix(query[:, at], [keys], [values], factor).astype(BF16)


def cross(queries, captions, block, factor):
    parts = len(queries)
    rows, columns = queries[0].shape
    total_keys = sum(c.shape[0] for c in captions) // 2
    return pl.pallas_call(
        lambda *refs: cross_kernel(factor, block, parts, *refs),
        out_shape=[shape(rows, columns)] * parts,
        in_specs=[in_vmem()] * (parts + len(captions)),
        out_specs=[in_vmem()] * parts,
        cost_estimate=cost(
            4 * parts * rows * total_keys * columns,
            (2 * parts * rows + 2 * total_keys) * columns * 2,
            parts * rows * total_keys * columns // DH,
        ),
        name="cross",
    )(*queries, *captions)


def project_kernel(groups, heads, at_ref, *refs):
    lhs, w_ref, out = refs[: groups * heads], refs[-2], refs[-1]
    width = heads * DH
    columns = out.shape[1]
    first = pl.multiple_of(at_ref[1] * columns, DH)
    block = math.gcd(columns, 512)
    lefts = [
        jnp.concatenate([lhs[r * heads + h][...] for h in range(heads)], axis=1)
        for r in range(groups)
    ]
    for n in range(columns // block):
        at = pl.ds(pl.multiple_of(first + n * block, DH), block)
        total = None
        for r in range(groups):
            base = pl.multiple_of(lax.rem(at_ref[0] + r, groups) * width, DH)
            term = jnp.dot(lefts[r], w_ref[pl.ds(base, width), at], preferred_element_type=F32)
            total = term if total is None else total + term
        out[:, n * block : (n + 1) * block] = total.astype(out.dtype)


def project(groups, at, lhs, weight, columns, dtype, name):
    heads = len(lhs) // groups
    rows = lhs[0].shape[0]
    depth = weight.shape[0]
    return pl.pallas_call(
        lambda *refs: project_kernel(groups, heads, *refs),
        out_shape=shape(rows, columns, dtype),
        in_specs=[in_smem()] + [in_vmem()] * (len(lhs) + 1),
        out_specs=in_vmem(),
        cost_estimate=cost(
            2 * rows * depth * columns, depth * columns * 2 + rows * columns * 4
        ),
        name=name,
    )(at, *lhs, weight)


def finish_kernel(at_ref, tokens, gate, home, away, stay, came, updated, cross_heads):
    projected = home[...] + away[...].astype(F32)
    updated[...] = (tokens[...].astype(F32) + gate[...] * projected).astype(BF16)
    half = stay.shape[1]
    for side, half_heads in ((at_ref[1], stay), (1 - at_ref[1], came)):
        cross_heads[:, pl.ds(pl.multiple_of(side * half, DH), half)] = half_heads[...]


def finish(at, tokens, gate, home, away, stay, came):
    return pl.pallas_call(
        finish_kernel,
        out_shape=[shape(*tokens.shape), shape(stay.shape[0], 2 * stay.shape[1])],
        in_specs=[in_smem()] + [in_vmem()] * 6,
        out_specs=[in_vmem()] * 2,
        cost_estimate=cost(0, tokens.size * 10),
        name="finish",
    )(at, tokens, gate[None, :], home, away, stay, came)


def shards(
    seq_size,
    tp_size,
    tokens,
    self_queries,
    self_keys,
    self_values,
    cross_queries,
    caption_keys,
    caption_values,
    out_weight,
    gate_vector,
):
    rows, columns = self_queries.shape
    heads_here = columns // DH
    factor = LOG2E / math.sqrt(DH)
    groups = math.gcd(heads_here, seq_size)
    members = seq_size // groups
    heads = heads_here // groups
    bit = members // 2
    split = members == 4 and heads_here % 2 == 0 and tp_size == 2
    seqi = lax.axis_index("seq").astype(jnp.int32)
    tpi = lax.axis_index("tp").astype(jnp.int32)
    zi = seqi // members
    place = jnp.stack([zi, (seqi // max(bit, 1)) % 2])

    def rotate(x, r):
        if r % groups == 0:
            return x
        step = (r % groups) * members
        return lax.ppermute(x, "seq", [(s, (s + step) % seq_size) for s in range(seq_size)])

    def swap(x, by):
        return lax.ppermute(x, "seq", [(s, s ^ by) for s in range(seq_size)])

    def spread(x):
        if members == 4:
            near = swap(x, 1)
            far = swap(x, 2)
            return [x, near, far, swap(far, 1)]
        index_groups = [[g * members + m for m in range(members)] for g in range(groups)]
        return [
            lax.all_gather(x, "seq", axis=0, tiled=True, axis_index_groups=index_groups)
        ]

    pieces = pack(groups, place, self_queries, self_keys, self_values)
    if split:
        q_stay, q_go, c_stay, c_go = pack_cross(
            place, cross_queries, caption_keys, caption_values
        )

    mixed = []
    arrived = []
    for h in range(heads):
        here = [pieces[r][h] for r in range(groups)]
        if h >= 2:
            here[1:] = [after(x, arrived[h - 2][1:]) for x in here[1:]]
        here = [rotate(x, r) for r, x in enumerate(here)]
        arrived.append(here)
        mine = jnp.concatenate([x[:, DH:] for x in here], axis=0)
        outs = attend(here, spread(mine), factor, "attend_%d" % h)
        mixed.append([rotate(x, groups - r) for r, x in enumerate(outs)])

    lhs = [mixed[h][r] for r in range(groups) for h in range(heads)]
    out_columns = tokens.shape[1]
    cap_rows = caption_keys.shape[0]
    if split:
        q_come, c_come = swap(q_go, bit), swap(c_go, bit)
        caption = jnp.concatenate([c_stay, c_come], axis=0)
        caption = after(caption, arrived[-1][1:])
        caption = jnp.concatenate([rotate(caption, r) for r in range(groups)], axis=0)
        captions = [caption, swap(caption, 1)]
        stay, go = cross([q_stay, q_come], captions, cap_rows, factor)
        came = swap(go, bit)
        away = project(
            groups, jnp.stack([zi, 1 - tpi]), lhs, out_weight, out_columns, BF16, "away"
        )
        away = lax.ppermute(away, "tp", [(0, 1), (1, 0)])
        home = project(groups, jnp.stack([zi, tpi]), lhs, out_weight, out_columns, F32, "home")
        return tuple(finish(place, tokens, gate_vector, home, away, stay, came))

    caption = jnp.concatenate([caption_keys, caption_values], axis=0)
    caption = jnp.concatenate([rotate(caption, r) for r in range(groups)], axis=0)
    (cross_heads,) = cross([cross_queries], spread(caption), cap_rows, factor)
    both = project(
        groups, jnp.stack([zi, 0 * tpi]), lhs, out_weight, out_weight.shape[1], BF16, "both"
    )
    projected = lax.psum_scatter(both, "tp", scatter_dimension=1, tiled=True).astype(F32)
    updated = (tokens.astype(F32) + gate_vector[None, :] * projected).astype(BF16)
    return (updated, cross_heads)


def solution(mesh):
    seq_size, tp_size = mesh.shape["seq"], mesh.shape["tp"]
    return jax.shard_map(
        lambda *args: shards(seq_size, tp_size, *args),
        mesh=mesh,
        in_specs=(
            P("seq", "tp"),
            P("seq", "tp"),
            P("seq", "tp"),
            P("seq", "tp"),
            P("seq", "tp"),
            P("seq", "tp"),
            P("seq", "tp"),
            P("tp", None),
            P("tp"),
        ),
        out_specs=(P("seq", "tp"), P("seq", "tp")),
        check_vma=False,
    )
```

```python
import math

import jax
import jax.numpy as jnp
from jax import lax
from jax.experimental import pallas as pl
from jax.experimental.pallas import tpu as pltpu
from jax.sharding import PartitionSpec as P

DH = 128
F32 = jnp.float32
BF16 = jnp.bfloat16
LOG2E = 1.4426950408889634


def in_vmem():
    return pl.BlockSpec(memory_space=pltpu.VMEM)


def anywhere():
    return pl.BlockSpec(memory_space=pl.ANY)


def limit(mebibytes):
    return pltpu.CompilerParams(vmem_limit_bytes=mebibytes * 2**20)


def cost(flops, nbytes, transcendentals=0):
    return pl.CostEstimate(
        flops=int(flops), bytes_accessed=int(nbytes), transcendentals=int(transcendentals)
    )


def shape(rows, columns, dtype=BF16):
    return jax.ShapeDtypeStruct((rows, columns), dtype)


def after(x, *others):
    return lax.optimization_barrier((x, others))[0]


def softmax_mix(query, keys, values, factor):
    scores = [
        lax.dot_general(query, block, (((1,), (1,)), ((), ())), preferred_element_type=F32)
        for block in keys
    ]
    top = jnp.max(scores[0], axis=1, keepdims=True)
    for block in scores[1:]:
        top = jnp.maximum(top, jnp.max(block, axis=1, keepdims=True))
    total = None
    mixed = None
    for block, value in zip(scores, values):
        weight = jnp.exp2((block - top) * factor)
        part = jnp.sum(weight, axis=1, keepdims=True)
        total = part if total is None else total + part
        term = jnp.dot(weight.astype(BF16), value, preferred_element_type=F32)
        mixed = term if mixed is None else mixed + term
    return mixed / total


def copy_all(pairs, sems):
    copies = [
        pltpu.make_async_copy(source, target, sems.at[i])
        for i, (source, target) in enumerate(pairs)
    ]
    for copy in copies:
        copy.start()
    for copy in copies:
        copy.wait()


def pack(groups, members, chosen, q, k, v):
    rows, columns = q.shape
    width = columns // groups
    count = groups * len(chosen)

    def kernel(*refs):
        sources, outs, sems = refs[:3], refs[3:-1], refs[-1]
        zi = lax.axis_index("seq") // members
        pairs = []
        for j, h in enumerate(chosen):
            for r in range(groups):
                at = pl.ds(pl.multiple_of(lax.rem(zi + r, groups) * width + h * DH, DH), DH)
                for i, source in enumerate(sources):
                    target = outs[j * groups + r].at[:, i * DH : (i + 1) * DH]
                    pairs.append((source.at[:, at], target))
        copy_all(pairs, sems)

    outs = pl.pallas_call(
        kernel,
        out_shape=[shape(rows, 3 * DH)] * count,
        in_specs=[anywhere()] * 3,
        out_specs=[anywhere()] * count,
        scratch_shapes=[pltpu.SemaphoreType.DMA((3 * count,))],
        compiler_params=limit(1),
        cost_estimate=cost(0, 6 * count * rows * DH * 2),
        name="pack_%d" % chosen[0],
    )(q, k, v)
    return [list(outs[j * groups : (j + 1) * groups]) for j in range(len(chosen))]


def pack_cross(bit, q, k, v):
    rows, columns = q.shape
    half = columns // 2
    total = rows + 2 * k.shape[0]

    def kernel(*refs):
        sources, outs, sems = refs[:3], refs[3:5], refs[5]
        xi = lax.rem(lax.axis_index("seq") // bit, 2)
        pairs = []
        for out, side in zip(outs, (xi, 1 - xi)):
            at = pl.ds(pl.multiple_of(side * half, DH), half)
            first = 0
            for source in sources:
                last = first + source.shape[0]
                pairs.append((source.at[:, at], out.at[first:last, :]))
                first = last
        copy_all(pairs, sems)

    return pl.pallas_call(
        kernel,
        out_shape=[shape(total, half)] * 2,
        in_specs=[anywhere()] * 3,
        out_specs=[anywhere()] * 2,
        scratch_shapes=[pltpu.SemaphoreType.DMA((6,))],
        compiler_params=limit(1),
        cost_estimate=cost(0, 4 * total * columns),
        name="pack_cross",
    )(q, k, v)


def attend(queries, pairs, earlier, factor, name):
    parts = len(queries)
    rows = queries[0].shape[0]
    before = earlier[0].shape[1] if earlier else 0
    total_keys = sum(p.shape[0] for p in pairs)

    def kernel(*refs):
        query_refs, refs = refs[:parts], refs[parts:]
        pair_refs, refs = refs[: len(pairs)], refs[len(pairs) :]
        early, outs = refs[:-parts], refs[-parts:]
        keys = [ref[:, :DH] for ref in pair_refs]
        values = [ref[:, DH:] for ref in pair_refs]
        for i in range(parts):
            if before:
                outs[i][:, :before] = early[i][...]
            outs[i][:, before:] = softmax_mix(
                query_refs[i][:, :DH], keys, values, factor
            ).astype(BF16)

    return pl.pallas_call(
        kernel,
        out_shape=[shape(rows, before + DH)] * parts,
        in_specs=[in_vmem()] * (parts + len(pairs) + len(earlier)),
        out_specs=[in_vmem()] * parts,
        compiler_params=limit(14),
        cost_estimate=cost(
            4 * parts * rows * total_keys * DH, total_keys * DH * 4, parts * rows * total_keys
        ),
        name=name,
    )(*queries, *pairs, *earlier)


def cross(queries, captions, rows, block, factor):
    parts = len(queries)
    columns = queries[0].shape[1]
    total_keys = sum(c.shape[0] for c in captions) // 2

    def kernel(*refs):
        query_refs, caption_refs, outs = refs[:parts], refs[parts:-parts], refs[-parts:]
        for h in range(columns // DH):
            at = slice(h * DH, (h + 1) * DH)
            keys, values = [
                jnp.concatenate(
                    [
                        c[b * block : (b + 1) * block, at]
                        for c in caption_refs
                        for b in range(first, c.shape[0] // block, 2)
                    ],
                    axis=0,
                )
                for first in (0, 1)
            ]
            for query, out in zip(query_refs, outs):
                out[:, at] = softmax_mix(query[:rows, at], [keys], [values], factor).astype(
                    BF16
                )

    return pl.pallas_call(
        kernel,
        out_shape=[shape(rows, columns)] * parts,
        in_specs=[in_vmem()] * (parts + len(captions)),
        out_specs=[in_vmem()] * parts,
        compiler_params=limit(14),
        cost_estimate=cost(
            4 * parts * rows * total_keys * columns,
            (2 * parts * rows + 2 * total_keys) * columns * 2,
            parts * rows * total_keys * columns // DH,
        ),
        name="cross",
    )(*queries, *captions)


def project(members, tp_size, turn, lhs, weight, dtype, name):
    groups = len(lhs)
    rows, width = lhs[0].shape
    depth = weight.shape[0]
    columns = weight.shape[1] // tp_size

    def kernel(*refs):
        lhs_refs, w_ref, out = refs[:groups], refs[-2], refs[-1]
        zi = lax.axis_index("seq") // members
        side = lax.rem(lax.axis_index("tp") + turn, tp_size) if tp_size > 1 else 0
        block = math.gcd(columns, 512)
        for n in range(columns // block):
            at = pl.ds(pl.multiple_of(side * columns + n * block, DH), block)
            total = None
            for r in range(groups):
                base = pl.multiple_of(lax.rem(zi + r, groups) * width, DH)
                term = jnp.dot(
                    lhs_refs[r][...], w_ref[pl.ds(base, width), at], preferred_element_type=F32
                )
                total = term if total is None else total + term
            out[:, n * block : (n + 1) * block] = total.astype(out.dtype)

    return pl.pallas_call(
        kernel,
        out_shape=shape(rows, columns, dtype),
        in_specs=[in_vmem()] * (groups + 1),
        out_specs=in_vmem(),
        compiler_params=limit(24),
        cost_estimate=cost(
            2 * rows * depth * columns, depth * columns * 2 + rows * columns * 4
        ),
        name=name,
    )(*lhs, weight)


def finish(bit, tokens, gate, home, away, stay, came):
    def kernel(tokens, gate, home, away, stay, came, updated, cross_heads):
        projected = home[...] + away[...].astype(F32)
        updated[...] = (tokens[...].astype(F32) + gate[...] * projected).astype(BF16)
        half = stay.shape[1]
        xi = lax.rem(lax.axis_index("seq") // bit, 2)
        for side, half_heads in ((xi, stay), (1 - xi, came)):
            cross_heads[:, pl.ds(pl.multiple_of(side * half, DH), half)] = half_heads[...]

    return pl.pallas_call(
        kernel,
        out_shape=[shape(*tokens.shape), shape(stay.shape[0], 2 * stay.shape[1])],
        in_specs=[in_vmem()] * 6,
        out_specs=[in_vmem()] * 2,
        compiler_params=limit(12),
        cost_estimate=cost(0, tokens.size * 10),
        name="finish",
    )(tokens, gate[None, :], home, away, stay, came)


def shards(
    seq_size,
    tp_size,
    tokens,
    self_queries,
    self_keys,
    self_values,
    cross_queries,
    caption_keys,
    caption_values,
    out_weight,
    gate_vector,
):
    rows, columns = self_queries.shape
    heads_here = columns // DH
    factor = LOG2E / math.sqrt(DH)
    groups = math.gcd(heads_here, seq_size)
    members = seq_size // groups
    heads = heads_here // groups
    bit = members // 2
    cap_rows = caption_keys.shape[0]

    def rotate(x, r):
        if r % groups == 0:
            return x
        step = (r % groups) * members
        return lax.ppermute(x, "seq", [(s, (s + step) % seq_size) for s in range(seq_size)])

    def swap(x, by):
        return lax.ppermute(x, "seq", [(s, s ^ by) for s in range(seq_size)])

    def join(*xs):
        return xs[0] if len(xs) == 1 else jnp.concatenate(xs, axis=0)

    if members != 4 or heads_here % 2 or tp_size != 2:
        index_groups = [[g * members + m for m in range(members)] for g in range(groups)]

        def gather(x):
            return lax.all_gather(
                x, "seq", axis=0, tiled=True, axis_index_groups=index_groups
            )

        pieces = pack(groups, members, range(heads), self_queries, self_keys, self_values)
        outs = []
        for h in range(heads):
            here = [rotate(x, r) for r, x in enumerate(pieces[h])]
            pair = gather(join(*[x[:, DH:] for x in here]))
            outs = attend(here, [pair], outs, factor, "attend_%d" % h)
        lhs = [rotate(x, groups - r) for r, x in enumerate(outs)]
        caption = join(caption_keys, caption_values)
        caption = gather(join(*[rotate(caption, r) for r in range(groups)]))
        (cross_heads,) = cross([cross_queries], [caption], rows, cap_rows, factor)
        both = project(members, 1, 0, lhs, out_weight, BF16, "both")
        projected = lax.psum_scatter(both, "tp", scatter_dimension=1, tiled=True).astype(F32)
        updated = (tokens.astype(F32) + gate_vector[None, :] * projected).astype(BF16)
        return (updated, cross_heads)

    pieces = pack(groups, members, [0], self_queries, self_keys, self_values)
    pieces += pack(
        groups, members, list(range(1, heads)), self_queries, self_keys, self_values
    )
    stay, go = pack_cross(bit, cross_queries, caption_keys, caption_values)
    outs, arrived, far = [], [], []
    for h in range(heads):
        here = pieces[h]
        if h >= 2:
            here = here[:1] + [after(x, arrived[h - 2][1:]) for x in here[1:]]
        here = [rotate(x, r) for r, x in enumerate(here)]
        arrived.append(here)
        mine = join(*[x[:, DH:] for x in here])
        far.append(swap(mine, 2))
        half = join(mine, far[h])
        outs = attend(here, [half, swap(half, 1)], outs, factor, "attend_%d" % h)
    lhs = [rotate(x, groups - r) for r, x in enumerate(outs)]

    come = swap(after(go, far[0]), bit)
    caption = after(join(stay[rows:], come[rows:]), arrived[-1][1:])
    caption = join(*[rotate(caption, r) for r in range(groups)])
    captions = [caption, swap(caption, 1)]

    away = project(members, tp_size, 1, lhs, out_weight, BF16, "away")
    captions[0] = after(captions[0], away)
    own, theirs = cross([stay, come], captions, rows, cap_rows, factor)
    came = swap(theirs, bit)
    away = lax.ppermute(away, "tp", [(0, 1), (1, 0)])
    home = project(members, tp_size, 0, lhs, out_weight, F32, "home")
    return tuple(finish(bit, tokens, gate_vector, home, away, own, came))


def solution(mesh):
    seq_size, tp_size = mesh.shape["seq"], mesh.shape["tp"]
    return jax.shard_map(
        lambda *args: shards(seq_size, tp_size, *args),
        mesh=mesh,
        in_specs=(
            P("seq", "tp"),
            P("seq", "tp"),
            P("seq", "tp"),
            P("seq", "tp"),
            P("seq", "tp"),
            P("seq", "tp"),
            P("seq", "tp"),
            P("tp", None),
            P("tp"),
        ),
        out_specs=(P("seq", "tp"), P("seq", "tp")),
        check_vma=False,
    )
```

```python
import math

import jax
import jax.numpy as jnp
from jax import lax
from jax.experimental import pallas as pl
from jax.experimental.pallas import tpu as pltpu
from jax.sharding import PartitionSpec as P

DH = 128
F32 = jnp.float32
BF16 = jnp.bfloat16
LOG2E = 1.4426950408889634


def in_vmem():
    return pl.BlockSpec(memory_space=pltpu.VMEM)


def anywhere():
    return pl.BlockSpec(memory_space=pl.ANY)


def in_hbm():
    return pl.BlockSpec(memory_space=pltpu.HBM)


def limit(mebibytes):
    return pltpu.CompilerParams(vmem_limit_bytes=mebibytes * 2**20)


def cost(flops, nbytes, transcendentals=0):
    return pl.CostEstimate(
        flops=int(flops), bytes_accessed=int(nbytes), transcendentals=int(transcendentals)
    )


def shape(rows, columns, dtype=BF16):
    return jax.ShapeDtypeStruct((rows, columns), dtype)


def after(x, *others):
    return lax.optimization_barrier((x, others))[0]


def softmax_mix(query, keys, values, factor):
    scores = [
        lax.dot_general(query, block, (((1,), (1,)), ((), ())), preferred_element_type=F32)
        for block in keys
    ]
    top = jnp.max(scores[0], axis=1, keepdims=True)
    for block in scores[1:]:
        top = jnp.maximum(top, jnp.max(block, axis=1, keepdims=True))
    total = None
    mixed = None
    for block, value in zip(scores, values):
        weight = jnp.exp2((block - top) * factor)
        part = jnp.sum(weight, axis=1, keepdims=True)
        total = part if total is None else total + part
        term = jnp.dot(weight.astype(BF16), value, preferred_element_type=F32)
        mixed = term if mixed is None else mixed + term
    return mixed / total


def copy_all(pairs, sems):
    copies = [
        pltpu.make_async_copy(source, target, sems.at[i])
        for i, (source, target) in enumerate(pairs)
    ]
    for copy in copies:
        copy.start()
    for copy in copies:
        copy.wait()


def pack(name, out_shapes, sources, plan):
    count = len(plan(0))

    def kernel(*refs):
        source_refs, outs, sems = refs[: len(sources)], refs[len(sources) : -1], refs[-1]
        pairs = []
        for i, at, width, o, row, column in plan(lax.axis_index("seq")):
            rows = source_refs[i].shape[0]
            if not isinstance(at, int):
                at = pl.multiple_of(at, DH)
            pairs.append(
                (
                    source_refs[i].at[:, pl.ds(at, width)],
                    outs[o].at[row : row + rows, column : column + width],
                )
            )
        copy_all(pairs, sems)

    return list(
        pl.pallas_call(
            kernel,
            out_shape=out_shapes,
            in_specs=[in_hbm()] * len(sources),
            out_specs=[anywhere()] * len(out_shapes),
            scratch_shapes=[pltpu.SemaphoreType.DMA((count,))],
            compiler_params=limit(1),
            cost_estimate=cost(0, 4 * sum(math.prod(o.shape) for o in out_shapes)),
            name=name,
        )(*[pltpu.with_memory_space_constraint(x, pltpu.HBM) for x in sources])
    )


def pack_pairs(groups, members, chosen, k, v):
    rows, columns = k.shape
    width = columns // groups

    def plan(seq):
        return [
            (i, lax.rem(seq // members + r, groups) * width + h * DH, DH, j * groups + r, 0, i * DH)
            for j, h in enumerate(chosen)
            for r in range(groups)
            for i in range(2)
        ]

    outs = pack(
        "pack_pairs_%d" % chosen[0],
        [shape(rows, 2 * DH)] * (groups * len(chosen)),
        [k, v],
        plan,
    )
    return [outs[j * groups : (j + 1) * groups] for j in range(len(chosen))]


def pack_queries(groups, members, q):
    rows, columns = q.shape
    width = columns // groups

    def plan(seq):
        return [
            (0, lax.rem(seq // members + r, groups) * width, width, r, 0, 0)
            for r in range(groups)
        ]

    return pack("pack_queries", [shape(rows, width)] * groups, [q], plan)


def pack_cross(bit, go, q, k, v):
    rows, columns = q.shape
    half = columns // 2
    more = k.shape[0]

    def plan(seq):
        xi = lax.rem(seq // bit, 2)
        at = ((1 - xi) if go else xi) * half
        return [
            (0, at, half, 0, 0, 0),
            (1, at, half, 0, rows, 0),
            (2, at, half, 0, rows + more, 0),
        ]

    name = "pack_go" if go else "pack_stay"
    return pack(name, [shape(rows + 2 * more, half)], [q, k, v], plan)[0]


def attend(queries, pairs, earlier, head, factor):
    parts = len(queries)
    rows = queries[0].shape[0]
    before = earlier[0].shape[1] if earlier else 0
    total_keys = sum(p.shape[0] for p in pairs)

    def kernel(*refs):
        query_refs, refs = refs[:parts], refs[parts:]
        pair_refs, refs = refs[: len(pairs)], refs[len(pairs) :]
        early, outs = refs[:-parts], refs[-parts:]
        keys = [ref[:, :DH] for ref in pair_refs]
        values = [ref[:, DH:] for ref in pair_refs]
        for i in range(parts):
            if before:
                outs[i][:, :before] = early[i][...]
            outs[i][:, before:] = softmax_mix(
                query_refs[i][:, head * DH : (head + 1) * DH], keys, values, factor
            ).astype(BF16)

    return pl.pallas_call(
        kernel,
        out_shape=[shape(rows, before + DH)] * parts,
        in_specs=[in_vmem()] * (parts + len(pairs) + len(earlier)),
        out_specs=[in_vmem()] * parts,
        compiler_params=limit(14),
        cost_estimate=cost(
            4 * parts * rows * total_keys * DH, total_keys * DH * 4, parts * rows * total_keys
        ),
        name="attend_%d" % head,
    )(*queries, *pairs, *earlier)


def cross(queries, captions, rows, block, factor):
    parts = len(queries)
    columns = queries[0].shape[1]
    total_keys = sum(c.shape[0] for c in captions) // 2

    def kernel(*refs):
        query_refs, caption_refs, outs = refs[:parts], refs[parts:-parts], refs[-parts:]
        for h in range(columns // DH):
            at = slice(h * DH, (h + 1) * DH)
            keys, values = [
                jnp.concatenate(
                    [
                        c[b * block : (b + 1) * block, at]
                        for c in caption_refs
                        for b in range(first, c.shape[0] // block, 2)
                    ],
                    axis=0,
                )
                for first in (0, 1)
            ]
            for query, out in zip(query_refs, outs):
                out[:, at] = softmax_mix(query[:rows, at], [keys], [values], factor).astype(
                    BF16
                )

    return pl.pallas_call(
        kernel,
        out_shape=[shape(rows, columns)] * parts,
        in_specs=[in_vmem()] * (parts + len(captions)),
        out_specs=[in_vmem()] * parts,
        compiler_params=limit(14),
        cost_estimate=cost(
            4 * parts * rows * total_keys * columns,
            (2 * parts * rows + 2 * total_keys) * columns * 2,
            parts * rows * total_keys * columns // DH,
        ),
        name="cross",
    )(*queries, *captions)


def project(members, tp_size, turn, lhs, weight, dtype, name):
    groups = len(lhs)
    rows, width = lhs[0].shape
    depth = weight.shape[0]
    columns = weight.shape[1] // tp_size

    def kernel(*refs):
        lhs_refs, w_ref, out = refs[:groups], refs[-2], refs[-1]
        zi = lax.axis_index("seq") // members
        side = lax.rem(lax.axis_index("tp") + turn, tp_size) if tp_size > 1 else 0
        block = math.gcd(columns, 512)
        for n in range(columns // block):
            at = pl.ds(pl.multiple_of(side * columns + n * block, DH), block)
            total = None
            for r in range(groups):
                base = pl.multiple_of(lax.rem(zi + r, groups) * width, DH)
                term = jnp.dot(
                    lhs_refs[r][...], w_ref[pl.ds(base, width), at], preferred_element_type=F32
                )
                total = term if total is None else total + term
            out[:, n * block : (n + 1) * block] = total.astype(out.dtype)

    return pl.pallas_call(
        kernel,
        out_shape=shape(rows, columns, dtype),
        in_specs=[in_vmem()] * (groups + 1),
        out_specs=in_vmem(),
        compiler_params=limit(24),
        cost_estimate=cost(
            2 * rows * depth * columns, depth * columns * 2 + rows * columns * 4
        ),
        name=name,
    )(*lhs, weight)


def finish(bit, tokens, gate, home, away, stay, came):
    def kernel(tokens, gate, home, away, stay, came, updated, cross_heads):
        projected = home[...] + away[...].astype(F32)
        updated[...] = (tokens[...].astype(F32) + gate[...] * projected).astype(BF16)
        half = stay.shape[1]
        xi = lax.rem(lax.axis_index("seq") // bit, 2)
        for side, half_heads in ((xi, stay), (1 - xi, came)):
            cross_heads[:, pl.ds(pl.multiple_of(side * half, DH), half)] = half_heads[...]

    return pl.pallas_call(
        kernel,
        out_shape=[shape(*tokens.shape), shape(stay.shape[0], 2 * stay.shape[1])],
        in_specs=[in_vmem()] * 6,
        out_specs=[in_vmem()] * 2,
        compiler_params=limit(12),
        cost_estimate=cost(0, tokens.size * 10),
        name="finish",
    )(tokens, gate[None, :], home, away, stay, came)


def shards(
    seq_size,
    tp_size,
    tokens,
    self_queries,
    self_keys,
    self_values,
    cross_queries,
    caption_keys,
    caption_values,
    out_weight,
    gate_vector,
):
    rows, columns = self_queries.shape
    heads_here = columns // DH
    factor = LOG2E / math.sqrt(DH)
    groups = math.gcd(heads_here, seq_size)
    members = seq_size // groups
    heads = heads_here // groups
    bit = members // 2
    cap_rows = caption_keys.shape[0]

    def rotate(x, r):
        if r % groups == 0:
            return x
        step = (r % groups) * members
        return lax.ppermute(x, "seq", [(s, (s + step) % seq_size) for s in range(seq_size)])

    def swap(x, by):
        return lax.ppermute(x, "seq", [(s, s ^ by) for s in range(seq_size)])

    def join(*xs):
        return xs[0] if len(xs) == 1 else jnp.concatenate(xs, axis=0)

    if (groups, members, tp_size) != (4, 4, 2):
        index_groups = [[g * members + m for m in range(members)] for g in range(groups)]

        def gather(x):
            return lax.all_gather(
                x, "seq", axis=0, tiled=True, axis_index_groups=index_groups
            )

        pairs = pack_pairs(groups, members, range(heads), self_keys, self_values)
        queries = pack_queries(groups, members, self_queries)
        queries = [rotate(x, r) for r, x in enumerate(queries)]
        outs = []
        for h in range(heads):
            pair = gather(join(*[rotate(x, r) for r, x in enumerate(pairs[h])]))
            outs = attend(queries, [pair], outs, h, factor)
        lhs = [rotate(x, groups - r) for r, x in enumerate(outs)]
        caption = join(caption_keys, caption_values)
        caption = gather(join(*[rotate(caption, r) for r in range(groups)]))
        (cross_heads,) = cross([cross_queries], [caption], rows, cap_rows, factor)
        both = project(members, 1, 0, lhs, out_weight, BF16, "both")
        projected = lax.psum_scatter(both, "tp", scatter_dimension=1, tiled=True).astype(F32)
        updated = (tokens.astype(F32) + gate_vector[None, :] * projected).astype(BF16)
        return (updated, cross_heads)

    pairs = pack_pairs(groups, members, [0], self_keys, self_values)
    go = pack_cross(bit, True, cross_queries, caption_keys, caption_values)
    pairs += pack_pairs(groups, members, list(range(1, heads)), self_keys, self_values)
    queries = pack_queries(groups, members, self_queries)
    stay = pack_cross(bit, False, cross_queries, caption_keys, caption_values)

    come = swap(go, bit)
    arrived, gathered = [], []
    for h in range(heads + 1):
        last = h == heads
        here = queries if last else pairs[h]
        if h:
            here = here[:1] + after(here[1:], arrived[-1][1])
        here = [rotate(x, r) for r, x in enumerate(here)]
        arrived.append(here)
        if not last:
            mine = join(*here)
            half = join(mine, swap(mine, 2))
            gathered.append([half, swap(half, 1)])
    outs = []
    for h in range(heads):
        outs = attend(arrived[-1], gathered[h], outs, h, factor)
    lhs = [rotate(x, groups - r) for r, x in enumerate(outs)]

    caption = join(stay[rows:], come[rows:])
    pair = join(caption, swap(after(caption, arrived[0][1:]), members))
    inner = [(m + members * g, m + members * (3 - g)) for g in (1, 2) for m in range(members)]
    outer = [(m + members * g, m + members * e) for g, e in ((1, 0), (2, 3)) for m in range(members)]
    middle = lax.ppermute(after(pair, arrived[-1][1:]), "seq", inner)
    ends = lax.ppermute(after(middle, outs), "seq", outer)
    zi = lax.axis_index("seq") // members
    other = jnp.where((zi == 1) | (zi == 2), middle, ends)

    away = project(members, tp_size, 1, lhs, out_weight, BF16, "away")
    captions = [after(pair, away), swap(pair, 1), other, swap(other, 1)]
    own, theirs = cross([stay, come], captions, rows, cap_rows, factor)
    came = swap(theirs, bit)
    away = lax.ppermute(away, "tp", [(0, 1), (1, 0)])
    home = project(members, tp_size, 0, lhs, out_weight, F32, "home")
    return tuple(finish(bit, tokens, gate_vector, home, away, own, came))


def solution(mesh):
    seq_size, tp_size = mesh.shape["seq"], mesh.shape["tp"]
    return jax.shard_map(
        lambda *args: shards(seq_size, tp_size, *args),
        mesh=mesh,
        in_specs=(
            P("seq", "tp"),
            P("seq", "tp"),
            P("seq", "tp"),
            P("seq", "tp"),
            P("seq", "tp"),
            P("seq", "tp"),
            P("seq", "tp"),
            P("tp", None),
            P("tp"),
        ),
        out_specs=(P("seq", "tp"), P("seq", "tp")),
        check_vma=False,
    )
```

```python
import math

import jax
import jax.numpy as jnp
from jax import lax
from jax.experimental import pallas as pl
from jax.experimental.pallas import tpu as pltpu
from jax.sharding import PartitionSpec as P

DH = 128
F32 = jnp.float32
BF16 = jnp.bfloat16
LOG2E = 1.4426950408889634


def in_vmem():
    return pl.BlockSpec(memory_space=pltpu.VMEM)


def anywhere():
    return pl.BlockSpec(memory_space=pl.ANY)


def in_hbm():
    return pl.BlockSpec(memory_space=pltpu.HBM)


def limit(mebibytes):
    return pltpu.CompilerParams(vmem_limit_bytes=mebibytes * 2**20)


def cost(flops, nbytes, transcendentals=0):
    return pl.CostEstimate(
        flops=int(flops), bytes_accessed=int(nbytes), transcendentals=int(transcendentals)
    )


def shape(rows, columns, dtype=BF16):
    return jax.ShapeDtypeStruct((rows, columns), dtype)


def after(x, *others):
    return lax.optimization_barrier((x, others))[0]


def softmax_mix(query, keys, values, factor):
    scores = [
        lax.dot_general(query, block, (((1,), (1,)), ((), ())), preferred_element_type=F32)
        for block in keys
    ]
    top = jnp.max(scores[0], axis=1, keepdims=True)
    for block in scores[1:]:
        top = jnp.maximum(top, jnp.max(block, axis=1, keepdims=True))
    total = None
    mixed = None
    for block, value in zip(scores, values):
        weight = jnp.exp2((block - top) * factor)
        part = jnp.sum(weight, axis=1, keepdims=True)
        total = part if total is None else total + part
        term = jnp.dot(weight.astype(BF16), value, preferred_element_type=F32)
        mixed = term if mixed is None else mixed + term
    return mixed / total


def copy_all(pairs, sems):
    copies = [
        pltpu.make_async_copy(source, target, sems.at[i])
        for i, (source, target) in enumerate(pairs)
    ]
    for copy in copies:
        copy.start()
    for copy in copies:
        copy.wait()


def pack(name, out_shapes, sources, plan):
    count = len(plan(0))

    def kernel(*refs):
        source_refs, outs, sems = refs[: len(sources)], refs[len(sources) : -1], refs[-1]
        pairs = []
        for i, at, width, o, row, column in plan(lax.axis_index("seq")):
            rows = source_refs[i].shape[0]
            if not isinstance(at, int):
                at = pl.multiple_of(at, DH)
            pairs.append(
                (
                    source_refs[i].at[:, pl.ds(at, width)],
                    outs[o].at[row : row + rows, column : column + width],
                )
            )
        copy_all(pairs, sems)

    return list(
        pl.pallas_call(
            kernel,
            out_shape=out_shapes,
            in_specs=[in_hbm()] * len(sources),
            out_specs=[anywhere()] * len(out_shapes),
            scratch_shapes=[pltpu.SemaphoreType.DMA((count,))],
            compiler_params=limit(1),
            cost_estimate=cost(0, 4 * sum(math.prod(o.shape) for o in out_shapes)),
            name=name,
        )(*[pltpu.with_memory_space_constraint(x, pltpu.HBM) for x in sources])
    )


def pack_pairs(groups, members, chosen, k, v):
    rows, columns = k.shape
    width = columns // groups

    def plan(seq):
        return [
            (
                i,
                lax.rem(seq // members + r, groups) * width + h * DH,
                DH,
                r,
                0,
                (2 * j + i) * DH,
            )
            for j, h in enumerate(chosen)
            for r in range(groups)
            for i in range(2)
        ]

    return pack(
        "pack_pairs_%d" % chosen[0],
        [shape(rows, 2 * DH * len(chosen))] * groups,
        [k, v],
        plan,
    )


def pack_queries(groups, members, q):
    rows, columns = q.shape
    width = columns // groups

    def plan(seq):
        return [
            (0, lax.rem(seq // members + r, groups) * width, width, r, 0, 0)
            for r in range(groups)
        ]

    return pack("pack_queries", [shape(rows, width)] * groups, [q], plan)


def pack_cross(bit, go, q, k, v):
    rows, columns = q.shape
    half = columns // 2
    more = k.shape[0]

    def plan(seq):
        xi = lax.rem(seq // bit, 2)
        at = ((1 - xi) if go else xi) * half
        return [
            (0, at, half, 0, 0, 0),
            (1, at, half, 0, rows, 0),
            (2, at, half, 0, rows + more, 0),
        ]

    name = "pack_go" if go else "pack_stay"
    return pack(name, [shape(rows + 2 * more, half)], [q, k, v], plan)[0]


def attend(queries, pairs, earlier, chosen, factor):
    parts = len(queries)
    rows = queries[0].shape[0]
    before = earlier[0].shape[1] if earlier else 0
    total_keys = sum(p.shape[0] for p in pairs)
    heads = len(chosen)

    def kernel(*refs):
        query_refs, refs = refs[:parts], refs[parts:]
        pair_refs, refs = refs[: len(pairs)], refs[len(pairs) :]
        early, outs = refs[:-parts], refs[-parts:]
        if before:
            for i in range(parts):
                outs[i][:, :before] = early[i][...]
        for j, h in enumerate(chosen):
            keys = [ref[:, 2 * j * DH : (2 * j + 1) * DH] for ref in pair_refs]
            values = [ref[:, (2 * j + 1) * DH : (2 * j + 2) * DH] for ref in pair_refs]
            for i in range(parts):
                outs[i][:, before + j * DH : before + (j + 1) * DH] = softmax_mix(
                    query_refs[i][:, h * DH : (h + 1) * DH], keys, values, factor
                ).astype(BF16)

    return pl.pallas_call(
        kernel,
        out_shape=[shape(rows, before + heads * DH)] * parts,
        in_specs=[in_vmem()] * (parts + len(pairs) + len(earlier)),
        out_specs=[in_vmem()] * parts,
        compiler_params=limit(14),
        cost_estimate=cost(
            4 * heads * parts * rows * total_keys * DH,
            heads * total_keys * DH * 4,
            heads * parts * rows * total_keys,
        ),
        name="attend_%d" % chosen[0],
    )(*queries, *pairs, *earlier)


def cross(queries, captions, rows, block, factor):
    parts = len(queries)
    columns = queries[0].shape[1]
    total_keys = sum(c.shape[0] for c in captions) // 2

    def kernel(*refs):
        query_refs, caption_refs, outs = refs[:parts], refs[parts:-parts], refs[-parts:]
        for h in range(columns // DH):
            at = slice(h * DH, (h + 1) * DH)
            keys, values = [
                jnp.concatenate(
                    [
                        c[b * block : (b + 1) * block, at]
                        for c in caption_refs
                        for b in range(first, c.shape[0] // block, 2)
                    ],
                    axis=0,
                )
                for first in (0, 1)
            ]
            for query, out in zip(query_refs, outs):
                out[:, at] = softmax_mix(query[:rows, at], [keys], [values], factor).astype(
                    BF16
                )

    return pl.pallas_call(
        kernel,
        out_shape=[shape(rows, columns)] * parts,
        in_specs=[in_vmem()] * (parts + len(captions)),
        out_specs=[in_vmem()] * parts,
        compiler_params=limit(14),
        cost_estimate=cost(
            4 * parts * rows * total_keys * columns,
            (2 * parts * rows + 2 * total_keys) * columns * 2,
            parts * rows * total_keys * columns // DH,
        ),
        name="cross",
    )(*queries, *captions)


def project(members, tp_size, turn, lhs, weight, dtype, name):
    groups = len(lhs)
    rows, width = lhs[0].shape
    depth = weight.shape[0]
    columns = weight.shape[1] // tp_size

    def kernel(*refs):
        lhs_refs, w_ref, out = refs[:groups], refs[-2], refs[-1]
        zi = lax.axis_index("seq") // members
        side = lax.rem(lax.axis_index("tp") + turn, tp_size) if tp_size > 1 else 0
        block = math.gcd(columns, 512)
        for n in range(columns // block):
            at = pl.ds(pl.multiple_of(side * columns + n * block, DH), block)
            total = None
            for r in range(groups):
                base = pl.multiple_of(lax.rem(zi + r, groups) * width, DH)
                term = jnp.dot(
                    lhs_refs[r][...], w_ref[pl.ds(base, width), at], preferred_element_type=F32
                )
                total = term if total is None else total + term
            out[:, n * block : (n + 1) * block] = total.astype(out.dtype)

    return pl.pallas_call(
        kernel,
        out_shape=shape(rows, columns, dtype),
        in_specs=[in_vmem()] * (groups + 1),
        out_specs=in_vmem(),
        compiler_params=limit(24),
        cost_estimate=cost(
            2 * rows * depth * columns, depth * columns * 2 + rows * columns * 4
        ),
        name=name,
    )(*lhs, weight)


def finish(bit, tokens, gate, home, away, stay, came):
    def kernel(tokens, gate, home, away, stay, came, updated, cross_heads):
        projected = home[...] + away[...].astype(F32)
        updated[...] = (tokens[...].astype(F32) + gate[...] * projected).astype(BF16)
        half = stay.shape[1]
        xi = lax.rem(lax.axis_index("seq") // bit, 2)
        for side, half_heads in ((xi, stay), (1 - xi, came)):
            cross_heads[:, pl.ds(pl.multiple_of(side * half, DH), half)] = half_heads[...]

    return pl.pallas_call(
        kernel,
        out_shape=[shape(*tokens.shape), shape(stay.shape[0], 2 * stay.shape[1])],
        in_specs=[in_vmem()] * 6,
        out_specs=[in_vmem()] * 2,
        compiler_params=limit(12),
        cost_estimate=cost(0, tokens.size * 10),
        name="finish",
    )(tokens, gate[None, :], home, away, stay, came)


def shards(
    seq_size,
    tp_size,
    tokens,
    self_queries,
    self_keys,
    self_values,
    cross_queries,
    caption_keys,
    caption_values,
    out_weight,
    gate_vector,
):
    rows, columns = self_queries.shape
    heads_here = columns // DH
    factor = LOG2E / math.sqrt(DH)
    groups = math.gcd(heads_here, seq_size)
    members = seq_size // groups
    heads = heads_here // groups
    bit = members // 2
    cap_rows = caption_keys.shape[0]

    def rotate(x, r):
        if r % groups == 0:
            return x
        step = (r % groups) * members
        return lax.ppermute(x, "seq", [(s, (s + step) % seq_size) for s in range(seq_size)])

    def swap(x, by):
        return lax.ppermute(x, "seq", [(s, s ^ by) for s in range(seq_size)])

    def join(*xs):
        return xs[0] if len(xs) == 1 else jnp.concatenate(xs, axis=0)

    if (groups, members, tp_size) != (4, 4, 2):
        index_groups = [[g * members + m for m in range(members)] for g in range(groups)]

        def gather(x):
            return lax.all_gather(
                x, "seq", axis=0, tiled=True, axis_index_groups=index_groups
            )

        queries = pack_queries(groups, members, self_queries)
        queries = [rotate(x, r) for r, x in enumerate(queries)]
        outs = []
        for h in range(heads):
            pairs = pack_pairs(groups, members, [h], self_keys, self_values)
            pair = gather(join(*[rotate(x, r) for r, x in enumerate(pairs)]))
            outs = attend(queries, [pair], outs, [h], factor)
        lhs = [rotate(x, groups - r) for r, x in enumerate(outs)]
        caption = join(caption_keys, caption_values)
        caption = gather(join(*[rotate(caption, r) for r in range(groups)]))
        (cross_heads,) = cross([cross_queries], [caption], rows, cap_rows, factor)
        both = project(members, 1, 0, lhs, out_weight, BF16, "both")
        projected = lax.psum_scatter(both, "tp", scatter_dimension=1, tiled=True).astype(F32)
        updated = (tokens.astype(F32) + gate_vector[None, :] * projected).astype(BF16)
        return (updated, cross_heads)

    chunks = [list(range(heads - 1)), [heads - 1]]
    pieces = [pack_pairs(groups, members, chunks[0], self_keys, self_values)]
    go = pack_cross(bit, True, cross_queries, caption_keys, caption_values)
    pieces += [pack_pairs(groups, members, c, self_keys, self_values) for c in chunks[1:]]
    pieces.append(pack_queries(groups, members, self_queries))
    stay = pack_cross(bit, False, cross_queries, caption_keys, caption_values)

    come = swap(go, bit)
    arrived, gathered = [], []
    for i, here in enumerate(pieces):
        if i:
            here = here[:1] + after(here[1:], arrived[-1][1])
        here = [rotate(x, r) for r, x in enumerate(here)]
        arrived.append(here)
        if i < len(chunks):
            mine = join(*here)
            half = join(mine, swap(mine, 2))
            gathered.append([half, swap(half, 1)])
    outs = []
    for chunk, pairs in zip(chunks, gathered):
        outs = attend(arrived[-1], pairs, outs, chunk, factor)
    lhs = [rotate(x, groups - r) for r, x in enumerate(outs)]

    caption = join(stay[rows:], come[rows:])
    pair = join(caption, swap(after(caption, arrived[0][1:]), members))
    inner = [(m + members * g, m + members * (3 - g)) for g in (1, 2) for m in range(members)]
    outer = [(m + members * g, m + members * e) for g, e in ((1, 0), (2, 3)) for m in range(members)]
    middle = lax.ppermute(after(pair, arrived[-1][1:]), "seq", inner)
    ends = lax.ppermute(middle, "seq", outer)
    other = middle + ends

    away = project(members, tp_size, 1, lhs, out_weight, BF16, "away")
    captions = [after(pair, away), swap(pair, 1), other, swap(other, 1)]
    own, theirs = cross([stay, come], captions, rows, cap_rows, factor)
    came = swap(theirs, bit)
    away = lax.ppermute(away, "tp", [(0, 1), (1, 0)])
    home = project(members, tp_size, 0, lhs, out_weight, F32, "home")
    return tuple(finish(bit, tokens, gate_vector, home, away, own, came))


def solution(mesh):
    seq_size, tp_size = mesh.shape["seq"], mesh.shape["tp"]
    return jax.shard_map(
        lambda *args: shards(seq_size, tp_size, *args),
        mesh=mesh,
        in_specs=(
            P("seq", "tp"),
            P("seq", "tp"),
            P("seq", "tp"),
            P("seq", "tp"),
            P("seq", "tp"),
            P("seq", "tp"),
            P("seq", "tp"),
            P("tp", None),
            P("tp"),
        ),
        out_specs=(P("seq", "tp"), P("seq", "tp")),
        check_vma=False,
    )
```

```python
import math

import jax
import jax.numpy as jnp
from jax import lax
from jax.experimental import pallas as pl
from jax.experimental.pallas import tpu as pltpu
from jax.sharding import PartitionSpec as P

DH = 128
F32 = jnp.float32
BF16 = jnp.bfloat16
LOG2E = 1.4426950408889634


def in_vmem():
    return pl.BlockSpec(memory_space=pltpu.VMEM)


def anywhere():
    return pl.BlockSpec(memory_space=pl.ANY)


def in_hbm():
    return pl.BlockSpec(memory_space=pltpu.HBM)


def limit(mebibytes):
    return pltpu.CompilerParams(vmem_limit_bytes=mebibytes * 2**20)


def cost(flops, nbytes, transcendentals=0):
    return pl.CostEstimate(
        flops=int(flops), bytes_accessed=int(nbytes), transcendentals=int(transcendentals)
    )


def shape(rows, columns, dtype=BF16):
    return jax.ShapeDtypeStruct((rows, columns), dtype)


def after(x, *others):
    return lax.optimization_barrier((x, others))[0]


def softmax_mix(query, keys, values, factor):
    scores = [
        lax.dot_general(query, block, (((1,), (1,)), ((), ())), preferred_element_type=F32)
        for block in keys
    ]
    top = jnp.max(scores[0], axis=1, keepdims=True)
    for block in scores[1:]:
        top = jnp.maximum(top, jnp.max(block, axis=1, keepdims=True))
    total = None
    mixed = None
    for block, value in zip(scores, values):
        weight = jnp.exp2((block - top) * factor)
        part = jnp.sum(weight, axis=1, keepdims=True)
        total = part if total is None else total + part
        term = jnp.dot(weight.astype(BF16), value, preferred_element_type=F32)
        mixed = term if mixed is None else mixed + term
    return mixed / total


def copy_all(pairs, sems):
    copies = [
        pltpu.make_async_copy(source, target, sems.at[i])
        for i, (source, target) in enumerate(pairs)
    ]
    for copy in copies:
        copy.start()
    for copy in copies:
        copy.wait()


def pack(name, out_shapes, sources, plan):
    count = len(plan(0))

    def kernel(*refs):
        source_refs, outs, sems = refs[: len(sources)], refs[len(sources) : -1], refs[-1]
        pairs = []
        for i, at, width, o, row, column in plan(lax.axis_index("seq")):
            rows = source_refs[i].shape[0]
            if not isinstance(at, int):
                at = pl.multiple_of(at, DH)
            pairs.append(
                (
                    source_refs[i].at[:, pl.ds(at, width)],
                    outs[o].at[row : row + rows, column : column + width],
                )
            )
        copy_all(pairs, sems)

    return list(
        pl.pallas_call(
            kernel,
            out_shape=out_shapes,
            in_specs=[in_hbm()] * len(sources),
            out_specs=[anywhere()] * len(out_shapes),
            scratch_shapes=[pltpu.SemaphoreType.DMA((count,))],
            compiler_params=limit(1),
            cost_estimate=cost(0, 4 * sum(math.prod(o.shape) for o in out_shapes)),
            name=name,
        )(*[pltpu.with_memory_space_constraint(x, pltpu.HBM) for x in sources])
    )


def pack_pieces(groups, members, lists, sources, name):
    rows, columns = sources[0].shape
    width = columns // groups

    def plan(seq):
        return [
            (i, lax.rem(seq // members + r, groups) * width + h * DH, DH, n * groups + r, 0, j * DH)
            for n, blocks in enumerate(lists)
            for j, (i, h) in enumerate(blocks)
            for r in range(groups)
        ]

    outs = pack(
        name,
        [shape(rows, DH * len(blocks)) for blocks in lists for _ in range(groups)],
        sources,
        plan,
    )
    return [outs[n * groups : (n + 1) * groups] for n in range(len(lists))]


def pack_cross(bit, go, q, k, v):
    rows, columns = q.shape
    half = columns // 2
    more = k.shape[0]

    def plan(seq):
        xi = lax.rem(seq // bit, 2)
        at = ((1 - xi) if go else xi) * half
        return [
            (0, at, half, 0, 0, 0),
            (1, at, half, 0, rows, 0),
            (2, at, half, 0, rows + more, 0),
        ]

    name = "pack_go" if go else "pack_stay"
    return pack(name, [shape(rows + 2 * more, half)], [q, k, v], plan)[0]


def attend(queries, first, pairs, earlier, chosen, factor):
    parts = len(queries)
    rows = queries[0].shape[0]
    before = earlier[0].shape[1] if earlier else 0
    total_keys = sum(p.shape[0] for p in pairs)
    heads = len(chosen)

    def kernel(*refs):
        query_refs, refs = refs[:parts], refs[parts:]
        pair_refs, refs = refs[: len(pairs)], refs[len(pairs) :]
        early, outs = refs[:-parts], refs[-parts:]
        if before:
            for i in range(parts):
                outs[i][:, :before] = early[i][...]
        for j, h in enumerate(chosen):
            keys = [ref[:, 2 * j * DH : (2 * j + 1) * DH] for ref in pair_refs]
            values = [ref[:, (2 * j + 1) * DH : (2 * j + 2) * DH] for ref in pair_refs]
            at = first + h * DH
            for i in range(parts):
                outs[i][:, before + j * DH : before + (j + 1) * DH] = softmax_mix(
                    query_refs[i][:, at : at + DH], keys, values, factor
                ).astype(BF16)

    return pl.pallas_call(
        kernel,
        out_shape=[shape(rows, before + heads * DH)] * parts,
        in_specs=[in_vmem()] * (parts + len(pairs) + len(earlier)),
        out_specs=[in_vmem()] * parts,
        compiler_params=limit(14),
        cost_estimate=cost(
            4 * heads * parts * rows * total_keys * DH,
            heads * total_keys * DH * 4,
            heads * parts * rows * total_keys,
        ),
        name="attend_%d" % chosen[0],
    )(*queries, *pairs, *earlier)


def cross(queries, captions, rows, block, factor):
    parts = len(queries)
    columns = queries[0].shape[1]
    total_keys = sum(c.shape[0] for c in captions) // 2

    def kernel(*refs):
        query_refs, caption_refs, outs = refs[:parts], refs[parts:-parts], refs[-parts:]
        for h in range(columns // DH):
            at = slice(h * DH, (h + 1) * DH)
            keys, values = [
                jnp.concatenate(
                    [
                        c[b * block : (b + 1) * block, at]
                        for c in caption_refs
                        for b in range(first, c.shape[0] // block, 2)
                    ],
                    axis=0,
                )
                for first in (0, 1)
            ]
            for query, out in zip(query_refs, outs):
                out[:, at] = softmax_mix(query[:rows, at], [keys], [values], factor).astype(
                    BF16
                )

    return pl.pallas_call(
        kernel,
        out_shape=[shape(rows, columns)] * parts,
        in_specs=[in_vmem()] * (parts + len(captions)),
        out_specs=[in_vmem()] * parts,
        compiler_params=limit(14),
        cost_estimate=cost(
            4 * parts * rows * total_keys * columns,
            (2 * parts * rows + 2 * total_keys) * columns * 2,
            parts * rows * total_keys * columns // DH,
        ),
        name="cross",
    )(*queries, *captions)


def project(members, tp_size, turn, lhs, weight, dtype, name):
    groups = len(lhs)
    rows, width = lhs[0].shape
    depth = weight.shape[0]
    columns = weight.shape[1] // tp_size

    def kernel(*refs):
        lhs_refs, w_ref, out = refs[:groups], refs[-2], refs[-1]
        zi = lax.axis_index("seq") // members
        side = lax.rem(lax.axis_index("tp") + turn, tp_size) if tp_size > 1 else 0
        block = math.gcd(columns, 512)
        for n in range(columns // block):
            at = pl.ds(pl.multiple_of(side * columns + n * block, DH), block)
            total = None
            for r in range(groups):
                base = pl.multiple_of(lax.rem(zi + r, groups) * width, DH)
                term = jnp.dot(
                    lhs_refs[r][...], w_ref[pl.ds(base, width), at], preferred_element_type=F32
                )
                total = term if total is None else total + term
            out[:, n * block : (n + 1) * block] = total.astype(out.dtype)

    return pl.pallas_call(
        kernel,
        out_shape=shape(rows, columns, dtype),
        in_specs=[in_vmem()] * (groups + 1),
        out_specs=in_vmem(),
        compiler_params=limit(24),
        cost_estimate=cost(
            2 * rows * depth * columns, depth * columns * 2 + rows * columns * 4
        ),
        name=name,
    )(*lhs, weight)


def finish(bit, tokens, gate, home, away, stay, came):
    def kernel(tokens, gate, home, away, stay, came, updated, cross_heads):
        projected = home[...] + away[...].astype(F32)
        updated[...] = (tokens[...].astype(F32) + gate[...] * projected).astype(BF16)
        half = stay.shape[1]
        xi = lax.rem(lax.axis_index("seq") // bit, 2)
        for side, half_heads in ((xi, stay), (1 - xi, came)):
            cross_heads[:, pl.ds(pl.multiple_of(side * half, DH), half)] = half_heads[...]

    return pl.pallas_call(
        kernel,
        out_shape=[shape(*tokens.shape), shape(stay.shape[0], 2 * stay.shape[1])],
        in_specs=[in_vmem()] * 6,
        out_specs=[in_vmem()] * 2,
        compiler_params=limit(12),
        cost_estimate=cost(0, tokens.size * 10),
        name="finish",
    )(tokens, gate[None, :], home, away, stay, came)


def shards(
    seq_size,
    tp_size,
    tokens,
    self_queries,
    self_keys,
    self_values,
    cross_queries,
    caption_keys,
    caption_values,
    out_weight,
    gate_vector,
):
    rows, columns = self_queries.shape
    heads_here = columns // DH
    factor = LOG2E / math.sqrt(DH)
    groups = math.gcd(heads_here, seq_size)
    members = seq_size // groups
    heads = heads_here // groups
    bit = members // 2
    cap_rows = caption_keys.shape[0]

    def rotate(x, r):
        if r % groups == 0:
            return x
        step = (r % groups) * members
        return lax.ppermute(x, "seq", [(s, (s + step) % seq_size) for s in range(seq_size)])

    def swap(x, by):
        return lax.ppermute(x, "seq", [(s, s ^ by) for s in range(seq_size)])

    def join(*xs):
        return xs[0] if len(xs) == 1 else jnp.concatenate(xs, axis=0)

    sources = [self_keys, self_values, self_queries]
    if (groups, members, tp_size) != (4, 4, 2):
        index_groups = [[g * members + m for m in range(members)] for g in range(groups)]

        def gather(x):
            return lax.all_gather(
                x, "seq", axis=0, tiled=True, axis_index_groups=index_groups
            )

        outs = []
        for h in range(heads):
            blocks = [(0, h), (1, h), (2, h)]
            (pieces,) = pack_pieces(groups, members, [blocks], sources, "pack_%d" % h)
            pieces = [rotate(x, r) for r, x in enumerate(pieces)]
            pair = gather(join(*[x[:, : 2 * DH] for x in pieces]))
            outs = attend(pieces, (2 - h) * DH, [pair], outs, [h], factor)
        lhs = [rotate(x, groups - r) for r, x in enumerate(outs)]
        caption = join(caption_keys, caption_values)
        caption = gather(join(*[rotate(caption, r) for r in range(groups)]))
        (cross_heads,) = cross([cross_queries], [caption], rows, cap_rows, factor)
        both = project(members, 1, 0, lhs, out_weight, BF16, "both")
        projected = lax.psum_scatter(both, "tp", scatter_dimension=1, tiled=True).astype(F32)
        updated = (tokens.astype(F32) + gate_vector[None, :] * projected).astype(BF16)
        return (updated, cross_heads)

    chunks = [list(range(2)), list(range(2, heads))]
    kv = [[(i, h) for h in chunk for i in range(2)] for chunk in chunks]
    kv[1] += [(2, h) for h in range(heads)]
    first = pack_pieces(groups, members, kv[:1], sources, "pack_first")[0]
    go = pack_cross(bit, True, cross_queries, caption_keys, caption_values)
    (second,) = pack_pieces(groups, members, kv[1:], sources, "pack_later")
    stay = pack_cross(bit, False, cross_queries, caption_keys, caption_values)

    def travel(pieces, gates):
        return pieces[:1] + [
            rotate(x if g is None else after(x, g), r + 1)
            for r, (x, g) in enumerate(zip(pieces[1:], gates))
        ]

    come = swap(go, bit)
    first = travel(first, [None] * 3)
    second = travel(second, [None, (first[1], come), (first[1], come)])
    mine = join(*first)
    half_first = join(mine, swap(mine, 2))
    caption = join(stay[rows:], come[rows:])
    pair = join(caption, swap(after(caption, first[1:]), members))
    at = 2 * DH * len(chunks[1])
    mine = join(*[x[:, :at] for x in second])
    half_second = join(mine, swap(after(mine, pair), 2))
    pairs_first = [half_first, swap(half_first, 1)]
    outs = attend(second, at, pairs_first, [], chunks[0], factor)
    beyond = swap(after(caption, second[1:]), 2 * members)
    pairs_second = [half_second, swap(after(half_second, (outs, beyond)), 1)]
    outs = attend(second, at, pairs_second, outs, chunks[1], factor)
    last = swap(after(pair[2 * cap_rows * 2 :], beyond), 2 * members)
    other = join(beyond, last)
    lhs = [rotate(x, groups - r) for r, x in enumerate(outs)]

    away = project(members, tp_size, 1, lhs, out_weight, BF16, "away")
    captions = [after(pair, away), swap(after(pair, away), 1), other, swap(other, 1)]
    own, theirs = cross([stay, come], captions, rows, cap_rows, factor)
    came = swap(theirs, bit)
    away = lax.ppermute(away, "tp", [(0, 1), (1, 0)])
    home = project(members, tp_size, 0, lhs, out_weight, F32, "home")
    return tuple(finish(bit, tokens, gate_vector, home, away, own, came))


def solution(mesh):
    seq_size, tp_size = mesh.shape["seq"], mesh.shape["tp"]
    return jax.shard_map(
        lambda *args: shards(seq_size, tp_size, *args),
        mesh=mesh,
        in_specs=(
            P("seq", "tp"),
            P("seq", "tp"),
            P("seq", "tp"),
            P("seq", "tp"),
            P("seq", "tp"),
            P("seq", "tp"),
            P("seq", "tp"),
            P("tp", None),
            P("tp"),
        ),
        out_specs=(P("seq", "tp"), P("seq", "tp")),
        check_vma=False,
    )
```

```python
import math

import jax
import jax.numpy as jnp
from jax import lax
from jax.experimental import pallas as pl
from jax.experimental.pallas import tpu as pltpu
from jax.sharding import PartitionSpec as P

DH = 128
F32 = jnp.float32
BF16 = jnp.bfloat16
LOG2E = 1.4426950408889634


def in_vmem():
    return pl.BlockSpec(memory_space=pltpu.VMEM)


def anywhere():
    return pl.BlockSpec(memory_space=pl.ANY)


def in_hbm():
    return pl.BlockSpec(memory_space=pltpu.HBM)


def limit(mebibytes):
    return pltpu.CompilerParams(vmem_limit_bytes=mebibytes * 2**20)


def cost(flops, nbytes, transcendentals=0):
    return pl.CostEstimate(
        flops=int(flops), bytes_accessed=int(nbytes), transcendentals=int(transcendentals)
    )


def shape(rows, columns, dtype=BF16):
    return jax.ShapeDtypeStruct((rows, columns), dtype)


def after(x, *others):
    return lax.optimization_barrier((x, others))[0]


def softmax_mix(query, keys, values, factor):
    scores = [
        lax.dot_general(query, block, (((1,), (1,)), ((), ())), preferred_element_type=F32)
        for block in keys
    ]
    top = jnp.max(scores[0], axis=1, keepdims=True)
    for block in scores[1:]:
        top = jnp.maximum(top, jnp.max(block, axis=1, keepdims=True))
    total = None
    mixed = None
    for block, value in zip(scores, values):
        weight = jnp.exp2((block - top) * factor)
        part = jnp.sum(weight, axis=1, keepdims=True)
        total = part if total is None else total + part
        term = jnp.dot(weight.astype(BF16), value, preferred_element_type=F32)
        mixed = term if mixed is None else mixed + term
    return mixed / total


def copy_all(pairs, sems):
    copies = [
        pltpu.make_async_copy(source, target, sems.at[i])
        for i, (source, target) in enumerate(pairs)
    ]
    for copy in copies:
        copy.start()
    for copy in copies:
        copy.wait()


def pack(name, out_shapes, sources, plan):
    count = len(plan(0))

    def kernel(*refs):
        source_refs, outs, sems = refs[: len(sources)], refs[len(sources) : -1], refs[-1]
        pairs = []
        for i, at, width, o, row, column in plan(lax.axis_index("seq")):
            rows = source_refs[i].shape[0]
            if not isinstance(at, int):
                at = pl.multiple_of(at, DH)
            pairs.append(
                (
                    source_refs[i].at[:, pl.ds(at, width)],
                    outs[o].at[row : row + rows, column : column + width],
                )
            )
        copy_all(pairs, sems)

    return list(
        pl.pallas_call(
            kernel,
            out_shape=out_shapes,
            in_specs=[in_hbm()] * len(sources),
            out_specs=[anywhere()] * len(out_shapes),
            scratch_shapes=[pltpu.SemaphoreType.DMA((count,))],
            compiler_params=limit(1),
            cost_estimate=cost(0, 4 * sum(math.prod(o.shape) for o in out_shapes)),
            name=name,
        )(*[pltpu.with_memory_space_constraint(x, pltpu.HBM) for x in sources])
    )


def pack_pieces(groups, members, lists, sources, name):
    rows, columns = sources[0].shape
    width = columns // groups

    def plan(seq):
        return [
            (i, lax.rem(seq // members + r, groups) * width + h * DH, DH, n * groups + r, 0, j * DH)
            for n, blocks in enumerate(lists)
            for j, (i, h) in enumerate(blocks)
            for r in range(groups)
        ]

    outs = pack(
        name,
        [shape(rows, DH * len(blocks)) for blocks in lists for _ in range(groups)],
        sources,
        plan,
    )
    return [outs[n * groups : (n + 1) * groups] for n in range(len(lists))]


def pack_cross(bit, go, q, k, v):
    rows, columns = q.shape
    half = columns // 2
    more = k.shape[0]

    def plan(seq):
        xi = lax.rem(seq // bit, 2)
        at = ((1 - xi) if go else xi) * half
        return [
            (0, at, half, 0, 0, 0),
            (1, at, half, 0, rows, 0),
            (2, at, half, 0, rows + more, 0),
        ]

    name = "pack_go" if go else "pack_stay"
    return pack(name, [shape(rows + 2 * more, half)], [q, k, v], plan)[0]


def attend(queries, first, pairs, earlier, chosen, factor):
    parts = len(queries)
    rows = queries[0].shape[0]
    before = earlier[0].shape[1] if earlier else 0
    total_keys = sum(p.shape[0] for p in pairs)
    heads = len(chosen)

    def kernel(*refs):
        query_refs, refs = refs[:parts], refs[parts:]
        pair_refs, refs = refs[: len(pairs)], refs[len(pairs) :]
        early, outs = refs[:-parts], refs[-parts:]
        if before:
            for i in range(parts):
                outs[i][:, :before] = early[i][...]
        for j, h in enumerate(chosen):
            keys = [ref[:, 2 * j * DH : (2 * j + 1) * DH] for ref in pair_refs]
            values = [ref[:, (2 * j + 1) * DH : (2 * j + 2) * DH] for ref in pair_refs]
            at = first + h * DH
            for i in range(parts):
                outs[i][:, before + j * DH : before + (j + 1) * DH] = softmax_mix(
                    query_refs[i][:, at : at + DH], keys, values, factor
                ).astype(BF16)

    return pl.pallas_call(
        kernel,
        out_shape=[shape(rows, before + heads * DH)] * parts,
        in_specs=[in_vmem()] * (parts + len(pairs) + len(earlier)),
        out_specs=[in_vmem()] * parts,
        compiler_params=limit(14),
        cost_estimate=cost(
            4 * heads * parts * rows * total_keys * DH,
            heads * total_keys * DH * 4,
            heads * parts * rows * total_keys,
        ),
        name="attend_%d" % chosen[0],
    )(*queries, *pairs, *earlier)


def cross(queries, captions, rows, block, factor):
    parts = len(queries)
    columns = queries[0].shape[1]
    total_keys = sum(c.shape[0] for c in captions) // 2

    def kernel(*refs):
        query_refs, caption_refs, outs = refs[:parts], refs[parts:-parts], refs[-parts:]
        for h in range(columns // DH):
            at = slice(h * DH, (h + 1) * DH)
            keys, values = [
                jnp.concatenate(
                    [
                        c[b * block : (b + 1) * block, at]
                        for c in caption_refs
                        for b in range(first, c.shape[0] // block, 2)
                    ],
                    axis=0,
                )
                for first in (0, 1)
            ]
            for query, out in zip(query_refs, outs):
                out[:, at] = softmax_mix(query[:rows, at], [keys], [values], factor).astype(
                    BF16
                )

    return pl.pallas_call(
        kernel,
        out_shape=[shape(rows, columns)] * parts,
        in_specs=[in_vmem()] * (parts + len(captions)),
        out_specs=[in_vmem()] * parts,
        compiler_params=limit(14),
        cost_estimate=cost(
            4 * parts * rows * total_keys * columns,
            (2 * parts * rows + 2 * total_keys) * columns * 2,
            parts * rows * total_keys * columns // DH,
        ),
        name="cross",
    )(*queries, *captions)


def project(members, tp_size, turn, lhs, weight, dtype, name):
    groups = len(lhs)
    rows, width = lhs[0].shape
    depth = weight.shape[0]
    columns = weight.shape[1] // tp_size

    def kernel(*refs):
        lhs_refs, w_ref, out = refs[:groups], refs[-2], refs[-1]
        zi = lax.axis_index("seq") // members
        side = lax.rem(lax.axis_index("tp") + turn, tp_size) if tp_size > 1 else 0
        block = math.gcd(columns, 512)
        for n in range(columns // block):
            at = pl.ds(pl.multiple_of(side * columns + n * block, DH), block)
            total = None
            for r in range(groups):
                base = pl.multiple_of(lax.rem(zi + r, groups) * width, DH)
                term = jnp.dot(
                    lhs_refs[r][...], w_ref[pl.ds(base, width), at], preferred_element_type=F32
                )
                total = term if total is None else total + term
            out[:, n * block : (n + 1) * block] = total.astype(out.dtype)

    return pl.pallas_call(
        kernel,
        out_shape=shape(rows, columns, dtype),
        in_specs=[in_vmem()] * (groups + 1),
        out_specs=in_vmem(),
        compiler_params=limit(24),
        cost_estimate=cost(
            2 * rows * depth * columns, depth * columns * 2 + rows * columns * 4
        ),
        name=name,
    )(*lhs, weight)


def finish(bit, tokens, gate, home, away, stay, came):
    def kernel(tokens, gate, home, away, stay, came, updated, cross_heads):
        projected = home[...] + away[...].astype(F32)
        updated[...] = (tokens[...].astype(F32) + gate[...] * projected).astype(BF16)
        half = stay.shape[1]
        xi = lax.rem(lax.axis_index("seq") // bit, 2)
        for side, half_heads in ((xi, stay), (1 - xi, came)):
            cross_heads[:, pl.ds(pl.multiple_of(side * half, DH), half)] = half_heads[...]

    return pl.pallas_call(
        kernel,
        out_shape=[shape(*tokens.shape), shape(stay.shape[0], 2 * stay.shape[1])],
        in_specs=[in_vmem()] * 6,
        out_specs=[in_vmem()] * 2,
        compiler_params=limit(12),
        cost_estimate=cost(0, tokens.size * 10),
        name="finish",
    )(tokens, gate[None, :], home, away, stay, came)


def shards(
    seq_size,
    tp_size,
    tokens,
    self_queries,
    self_keys,
    self_values,
    cross_queries,
    caption_keys,
    caption_values,
    out_weight,
    gate_vector,
):
    rows, columns = self_queries.shape
    heads_here = columns // DH
    factor = LOG2E / math.sqrt(DH)
    groups = math.gcd(heads_here, seq_size)
    members = seq_size // groups
    heads = heads_here // groups
    bit = members // 2
    cap_rows = caption_keys.shape[0]

    def rotate(x, r):
        if r % groups == 0:
            return x
        step = (r % groups) * members
        return lax.ppermute(x, "seq", [(s, (s + step) % seq_size) for s in range(seq_size)])

    def swap(x, by):
        return lax.ppermute(x, "seq", [(s, s ^ by) for s in range(seq_size)])

    def join(*xs):
        return xs[0] if len(xs) == 1 else jnp.concatenate(xs, axis=0)

    sources = [self_keys, self_values, self_queries]
    if (groups, members, tp_size) != (4, 4, 2):
        index_groups = [[g * members + m for m in range(members)] for g in range(groups)]

        def gather(x):
            return lax.all_gather(
                x, "seq", axis=0, tiled=True, axis_index_groups=index_groups
            )

        outs = []
        for h in range(heads):
            blocks = [(0, h), (1, h), (2, h)]
            (pieces,) = pack_pieces(groups, members, [blocks], sources, "pack_%d" % h)
            pieces = [rotate(x, r) for r, x in enumerate(pieces)]
            pair = gather(join(*[x[:, : 2 * DH] for x in pieces]))
            outs = attend(pieces, (2 - h) * DH, [pair], outs, [h], factor)
        lhs = [rotate(x, groups - r) for r, x in enumerate(outs)]
        caption = join(caption_keys, caption_values)
        caption = gather(join(*[rotate(caption, r) for r in range(groups)]))
        (cross_heads,) = cross([cross_queries], [caption], rows, cap_rows, factor)
        both = project(members, 1, 0, lhs, out_weight, BF16, "both")
        projected = lax.psum_scatter(both, "tp", scatter_dimension=1, tiled=True).astype(F32)
        updated = (tokens.astype(F32) + gate_vector[None, :] * projected).astype(BF16)
        return (updated, cross_heads)

    chunks = [list(range(2)), list(range(2, heads))]
    kv = [[(i, h) for h in chunk for i in range(2)] for chunk in chunks]
    kv[1] += [(2, h) for h in range(heads)]
    first = pack_pieces(groups, members, kv[:1], sources, "pack_first")[0]
    go = pack_cross(bit, True, cross_queries, caption_keys, caption_values)
    (second,) = pack_pieces(groups, members, kv[1:], sources, "pack_later")
    stay = pack_cross(bit, False, cross_queries, caption_keys, caption_values)

    def travel(pieces, gates):
        return pieces[:1] + [
            rotate(x if g is None else after(x, g), r + 1)
            for r, (x, g) in enumerate(zip(pieces[1:], gates))
        ]

    come = swap(go, bit)
    first = travel(first, [None] * 3)
    second = travel(second, [None, (first[1], come), (first[1], come)])
    mine = join(*first)
    half_first = join(mine, swap(mine, 2))
    caption = join(stay[rows:], come[rows:])
    pair = join(caption, swap(after(caption, first[1:]), members))
    at = 2 * DH * len(chunks[1])
    mine = join(*[x[:, :at] for x in second])
    half_second = join(mine, swap(after(mine, pair), 2))
    pairs_first = [half_first, swap(half_first, 1)]
    outs = attend(second, at, pairs_first, [], chunks[0], factor)
    beyond = swap(after(caption, second[1:]), 2 * members)
    pairs_second = [half_second, swap(after(half_second, (outs, beyond)), 1)]
    outs = attend(second, at, pairs_second, outs, chunks[1], factor)
    last = swap(after(beyond, outs), members)
    other = join(beyond, last)
    lhs = [rotate(x, groups - r) for r, x in enumerate(outs)]

    away = project(members, tp_size, 1, lhs, out_weight, BF16, "away")
    captions = [after(pair, away), swap(after(pair, away), 1), other, swap(other, 1)]
    own, theirs = cross([stay, come], captions, rows, cap_rows, factor)
    came = swap(theirs, bit)
    away = lax.ppermute(away, "tp", [(0, 1), (1, 0)])
    home = project(members, tp_size, 0, lhs, out_weight, F32, "home")
    return tuple(finish(bit, tokens, gate_vector, home, away, own, came))


def solution(mesh):
    seq_size, tp_size = mesh.shape["seq"], mesh.shape["tp"]
    return jax.shard_map(
        lambda *args: shards(seq_size, tp_size, *args),
        mesh=mesh,
        in_specs=(
            P("seq", "tp"),
            P("seq", "tp"),
            P("seq", "tp"),
            P("seq", "tp"),
            P("seq", "tp"),
            P("seq", "tp"),
            P("seq", "tp"),
            P("tp", None),
            P("tp"),
        ),
        out_specs=(P("seq", "tp"), P("seq", "tp")),
        check_vma=False,
    )
```

```python
import math

import jax
import jax.numpy as jnp
from jax import lax
from jax.experimental import pallas as pl
from jax.experimental.pallas import tpu as pltpu
from jax.sharding import PartitionSpec as P

DH = 128
F32 = jnp.float32
BF16 = jnp.bfloat16
LOG2E = 1.4426950408889634


def in_vmem():
    return pl.BlockSpec(memory_space=pltpu.VMEM)


def anywhere():
    return pl.BlockSpec(memory_space=pl.ANY)


def in_hbm():
    return pl.BlockSpec(memory_space=pltpu.HBM)


def limit(mebibytes):
    return pltpu.CompilerParams(vmem_limit_bytes=mebibytes * 2**20)


def cost(flops, nbytes, transcendentals=0):
    return pl.CostEstimate(
        flops=int(flops), bytes_accessed=int(nbytes), transcendentals=int(transcendentals)
    )


def shape(rows, columns, dtype=BF16):
    return jax.ShapeDtypeStruct((rows, columns), dtype)


def after(x, *others):
    return lax.optimization_barrier((x, others))[0]


def softmax_mix(query, keys, values, factor):
    scores = [
        lax.dot_general(query, block, (((1,), (1,)), ((), ())), preferred_element_type=F32)
        for block in keys
    ]
    top = jnp.max(scores[0], axis=1, keepdims=True)
    for block in scores[1:]:
        top = jnp.maximum(top, jnp.max(block, axis=1, keepdims=True))
    total = None
    mixed = None
    for block, value in zip(scores, values):
        weight = jnp.exp2((block - top) * factor)
        part = jnp.sum(weight, axis=1, keepdims=True)
        total = part if total is None else total + part
        term = jnp.dot(weight.astype(BF16), value, preferred_element_type=F32)
        mixed = term if mixed is None else mixed + term
    return mixed / total


def copy_all(pairs, sems):
    copies = [
        pltpu.make_async_copy(source, target, sems.at[i])
        for i, (source, target) in enumerate(pairs)
    ]
    for copy in copies:
        copy.start()
    for copy in copies:
        copy.wait()


def pack(name, out_shapes, sources, plan):
    count = len(plan(0))

    def kernel(*refs):
        source_refs, outs, sems = refs[: len(sources)], refs[len(sources) : -1], refs[-1]
        pairs = []
        for i, at, width, o, row, column in plan(lax.axis_index("seq")):
            rows = source_refs[i].shape[0]
            if not isinstance(at, int):
                at = pl.multiple_of(at, DH)
            pairs.append(
                (
                    source_refs[i].at[:, pl.ds(at, width)],
                    outs[o].at[row : row + rows, column : column + width],
                )
            )
        copy_all(pairs, sems)

    return list(
        pl.pallas_call(
            kernel,
            out_shape=out_shapes,
            in_specs=[in_hbm()] * len(sources),
            out_specs=[anywhere()] * len(out_shapes),
            scratch_shapes=[pltpu.SemaphoreType.DMA((count,))],
            compiler_params=limit(1),
            cost_estimate=cost(0, 4 * sum(math.prod(o.shape) for o in out_shapes)),
            name=name,
        )(*[pltpu.with_memory_space_constraint(x, pltpu.HBM) for x in sources])
    )


def pack_pieces(groups, members, lists, sources, name):
    rows, columns = sources[0].shape
    width = columns // groups

    def plan(seq):
        return [
            (i, lax.rem(seq // members + r, groups) * width + h * DH, DH, n * groups + r, 0, j * DH)
            for n, blocks in enumerate(lists)
            for j, (i, h) in enumerate(blocks)
            for r in range(groups)
        ]

    outs = pack(
        name,
        [shape(rows, DH * len(blocks)) for blocks in lists for _ in range(groups)],
        sources,
        plan,
    )
    return [outs[n * groups : (n + 1) * groups] for n in range(len(lists))]


def pack_cross(bit, go, q, k, v):
    rows, columns = q.shape
    half = columns // 2
    more = k.shape[0]

    def plan(seq):
        xi = lax.rem(seq // bit, 2)
        at = ((1 - xi) if go else xi) * half
        return [
            (0, at, half, 0, 0, 0),
            (1, at, half, 0, rows, 0),
            (2, at, half, 0, rows + more, 0),
        ]

    name = "pack_go" if go else "pack_stay"
    return pack(name, [shape(rows + 2 * more, half)], [q, k, v], plan)[0]


def attend(queries, first, pairs, earlier, chosen, factor):
    parts = len(queries)
    rows = queries[0].shape[0]
    before = earlier[0].shape[1] if earlier else 0
    total_keys = sum(p.shape[0] for p in pairs)
    heads = len(chosen)

    def kernel(*refs):
        query_refs, refs = refs[:parts], refs[parts:]
        pair_refs, refs = refs[: len(pairs)], refs[len(pairs) :]
        early, outs = refs[:-parts], refs[-parts:]
        if before:
            for i in range(parts):
                outs[i][:, :before] = early[i][...]
        for j, h in enumerate(chosen):
            keys = [ref[:, 2 * j * DH : (2 * j + 1) * DH] for ref in pair_refs]
            values = [ref[:, (2 * j + 1) * DH : (2 * j + 2) * DH] for ref in pair_refs]
            at = first + h * DH
            for i in range(parts):
                outs[i][:, before + j * DH : before + (j + 1) * DH] = softmax_mix(
                    query_refs[i][:, at : at + DH], keys, values, factor
                ).astype(BF16)

    return pl.pallas_call(
        kernel,
        out_shape=[shape(rows, before + heads * DH)] * parts,
        in_specs=[in_vmem()] * (parts + len(pairs) + len(earlier)),
        out_specs=[in_vmem()] * parts,
        compiler_params=limit(14),
        cost_estimate=cost(
            4 * heads * parts * rows * total_keys * DH,
            heads * total_keys * DH * 4,
            heads * parts * rows * total_keys,
        ),
        name="attend_%d" % chosen[0],
    )(*queries, *pairs, *earlier)


def cross(queries, captions, rows, block, factor):
    parts = len(queries)
    columns = queries[0].shape[1]
    total_keys = sum(c.shape[0] for c in captions) // 2

    def kernel(*refs):
        query_refs, caption_refs, outs = refs[:parts], refs[parts:-parts], refs[-parts:]
        for h in range(columns // DH):
            at = slice(h * DH, (h + 1) * DH)
            keys, values = [
                jnp.concatenate(
                    [
                        c[b * block : (b + 1) * block, at]
                        for c in caption_refs
                        for b in range(first, c.shape[0] // block, 2)
                    ],
                    axis=0,
                )
                for first in (0, 1)
            ]
            for query, out in zip(query_refs, outs):
                out[:, at] = softmax_mix(query[:rows, at], [keys], [values], factor).astype(
                    BF16
                )

    return pl.pallas_call(
        kernel,
        out_shape=[shape(rows, columns)] * parts,
        in_specs=[in_vmem()] * (parts + len(captions)),
        out_specs=[in_vmem()] * parts,
        compiler_params=limit(14),
        cost_estimate=cost(
            4 * parts * rows * total_keys * columns,
            (2 * parts * rows + 2 * total_keys) * columns * 2,
            parts * rows * total_keys * columns // DH,
        ),
        name="cross",
    )(*queries, *captions)


def project(members, tp_size, turn, lhs, weight, dtype, name):
    groups = len(lhs)
    rows, width = lhs[0].shape
    depth = weight.shape[0]
    columns = weight.shape[1] // tp_size

    def kernel(*refs):
        lhs_refs, w_ref, out = refs[:groups], refs[-2], refs[-1]
        zi = lax.axis_index("seq") // members
        side = lax.rem(lax.axis_index("tp") + turn, tp_size) if tp_size > 1 else 0
        block = math.gcd(columns, 512)
        for n in range(columns // block):
            at = pl.ds(pl.multiple_of(side * columns + n * block, DH), block)
            total = None
            for r in range(groups):
                base = pl.multiple_of(lax.rem(zi + r, groups) * width, DH)
                term = jnp.dot(
                    lhs_refs[r][...], w_ref[pl.ds(base, width), at], preferred_element_type=F32
                )
                total = term if total is None else total + term
            out[:, n * block : (n + 1) * block] = total.astype(out.dtype)

    return pl.pallas_call(
        kernel,
        out_shape=shape(rows, columns, dtype),
        in_specs=[in_vmem()] * (groups + 1),
        out_specs=in_vmem(),
        compiler_params=limit(24),
        cost_estimate=cost(
            2 * rows * depth * columns, depth * columns * 2 + rows * columns * 4
        ),
        name=name,
    )(*lhs, weight)


def finish(bit, tokens, gate, home, away, stay, came):
    def kernel(tokens, gate, home, away, stay, came, updated, cross_heads):
        projected = home[...] + away[...].astype(F32)
        updated[...] = (tokens[...].astype(F32) + gate[...] * projected).astype(BF16)
        half = stay.shape[1]
        xi = lax.rem(lax.axis_index("seq") // bit, 2)
        for side, half_heads in ((xi, stay), (1 - xi, came)):
            cross_heads[:, pl.ds(pl.multiple_of(side * half, DH), half)] = half_heads[...]

    return pl.pallas_call(
        kernel,
        out_shape=[shape(*tokens.shape), shape(stay.shape[0], 2 * stay.shape[1])],
        in_specs=[in_vmem()] * 6,
        out_specs=[in_vmem()] * 2,
        compiler_params=limit(12),
        cost_estimate=cost(0, tokens.size * 10),
        name="finish",
    )(tokens, gate[None, :], home, away, stay, came)


def shards(
    seq_size,
    tp_size,
    tokens,
    self_queries,
    self_keys,
    self_values,
    cross_queries,
    caption_keys,
    caption_values,
    out_weight,
    gate_vector,
):
    rows, columns = self_queries.shape
    heads_here = columns // DH
    factor = LOG2E / math.sqrt(DH)
    groups = math.gcd(heads_here, seq_size)
    members = seq_size // groups
    heads = heads_here // groups
    bit = members // 2
    cap_rows = caption_keys.shape[0]

    def rotate(x, r):
        if r % groups == 0:
            return x
        step = (r % groups) * members
        return lax.ppermute(x, "seq", [(s, (s + step) % seq_size) for s in range(seq_size)])

    def swap(x, by):
        return lax.ppermute(x, "seq", [(s, s ^ by) for s in range(seq_size)])

    def join(*xs):
        return xs[0] if len(xs) == 1 else jnp.concatenate(xs, axis=0)

    sources = [self_keys, self_values, self_queries]
    if (groups, members, tp_size) != (4, 4, 2):
        index_groups = [[g * members + m for m in range(members)] for g in range(groups)]

        def gather(x):
            return lax.all_gather(
                x, "seq", axis=0, tiled=True, axis_index_groups=index_groups
            )

        outs = []
        for h in range(heads):
            blocks = [(0, h), (1, h), (2, h)]
            (pieces,) = pack_pieces(groups, members, [blocks], sources, "pack_%d" % h)
            pieces = [rotate(x, r) for r, x in enumerate(pieces)]
            pair = gather(join(*[x[:, : 2 * DH] for x in pieces]))
            outs = attend(pieces, (2 - h) * DH, [pair], outs, [h], factor)
        lhs = [rotate(x, groups - r) for r, x in enumerate(outs)]
        caption = join(caption_keys, caption_values)
        caption = gather(join(*[rotate(caption, r) for r in range(groups)]))
        (cross_heads,) = cross([cross_queries], [caption], rows, cap_rows, factor)
        both = project(members, 1, 0, lhs, out_weight, BF16, "both")
        projected = lax.psum_scatter(both, "tp", scatter_dimension=1, tiled=True).astype(F32)
        updated = (tokens.astype(F32) + gate_vector[None, :] * projected).astype(BF16)
        return (updated, cross_heads)

    chunks = [list(range(2)), list(range(2, heads))]
    kv = [[(i, h) for h in chunk for i in range(2)] for chunk in chunks]
    kv[1] += [(2, h) for h in range(heads)]
    first = pack_pieces(groups, members, kv[:1], sources, "pack_first")[0]
    go = pack_cross(bit, True, cross_queries, caption_keys, caption_values)
    (second,) = pack_pieces(groups, members, kv[1:], sources, "pack_later")
    stay = pack_cross(bit, False, cross_queries, caption_keys, caption_values)

    def travel(pieces, gates):
        return pieces[:1] + [
            rotate(x if g is None else after(x, g), r + 1)
            for r, (x, g) in enumerate(zip(pieces[1:], gates))
        ]

    come = swap(go, bit)
    first = travel(first, [None] * 3)
    second = travel(second, [come, (first[1], come), (first[1], come)])
    mine = join(*first)
    half_first = join(mine, swap(mine, 2))
    caption = join(stay[rows:], come[rows:])
    pair = join(caption, swap(after(caption, first[1:]), members))
    at = 2 * DH * len(chunks[1])
    mine = join(*[x[:, :at] for x in second])
    half_second = join(mine, swap(after(mine, pair), 2))
    pairs_first = [half_first, swap(half_first, 1)]
    outs = attend(second, at, pairs_first, [], chunks[0], factor)
    beyond = swap(after(caption, pair), 2 * members)
    pairs_second = [half_second, swap(after(half_second, (outs, beyond)), 1)]
    outs = attend(second, at, pairs_second, outs, chunks[1], factor)
    last = swap(after(beyond, pair), members)
    other = join(beyond, last)
    lhs = [rotate(x, groups - r) for r, x in enumerate(outs)]

    away = project(members, tp_size, 1, lhs, out_weight, BF16, "away")
    captions = [after(pair, away), swap(after(pair, away), 1), other, swap(other, 1)]
    own, theirs = cross([stay, come], captions, rows, cap_rows, factor)
    came = swap(theirs, bit)
    away = lax.ppermute(away, "tp", [(0, 1), (1, 0)])
    home = project(members, tp_size, 0, lhs, out_weight, F32, "home")
    return tuple(finish(bit, tokens, gate_vector, home, away, own, came))


def solution(mesh):
    seq_size, tp_size = mesh.shape["seq"], mesh.shape["tp"]
    return jax.shard_map(
        lambda *args: shards(seq_size, tp_size, *args),
        mesh=mesh,
        in_specs=(
            P("seq", "tp"),
            P("seq", "tp"),
            P("seq", "tp"),
            P("seq", "tp"),
            P("seq", "tp"),
            P("seq", "tp"),
            P("seq", "tp"),
            P("tp", None),
            P("tp"),
        ),
        out_specs=(P("seq", "tp"), P("seq", "tp")),
        check_vma=False,
    )
```

```python
import math

import jax
import jax.numpy as jnp
from jax import lax
from jax.experimental import pallas as pl
from jax.experimental.pallas import tpu as pltpu
from jax.sharding import PartitionSpec as P

DH = 128
F32 = jnp.float32
BF16 = jnp.bfloat16
LOG2E = 1.4426950408889634


def in_vmem():
    return pl.BlockSpec(memory_space=pltpu.VMEM)


def anywhere():
    return pl.BlockSpec(memory_space=pl.ANY)


def in_hbm():
    return pl.BlockSpec(memory_space=pltpu.HBM)


def limit(mebibytes):
    return pltpu.CompilerParams(vmem_limit_bytes=mebibytes * 2**20)


def cost(flops, nbytes, transcendentals=0):
    return pl.CostEstimate(
        flops=int(flops), bytes_accessed=int(nbytes), transcendentals=int(transcendentals)
    )


def shape(rows, columns, dtype=BF16):
    return jax.ShapeDtypeStruct((rows, columns), dtype)


def after(x, *others):
    return lax.optimization_barrier((x, others))[0]


def softmax_mix(query, keys, values, factor):
    scores = [
        lax.dot_general(query, block, (((1,), (1,)), ((), ())), preferred_element_type=F32)
        for block in keys
    ]
    top = jnp.max(scores[0], axis=1, keepdims=True)
    for block in scores[1:]:
        top = jnp.maximum(top, jnp.max(block, axis=1, keepdims=True))
    mixed = None
    for block, value in zip(scores, values):
        weight = jnp.exp2((block - top) * factor).astype(BF16)
        wide = jnp.concatenate([value, jnp.ones_like(value)], axis=1)
        term = jnp.dot(weight, wide, preferred_element_type=F32)
        mixed = term if mixed is None else mixed + term
    return mixed[:, :DH] / mixed[:, DH:]


def copy_all(pairs, sems):
    copies = [
        pltpu.make_async_copy(source, target, sems.at[i])
        for i, (source, target) in enumerate(pairs)
    ]
    for copy in copies:
        copy.start()
    for copy in copies:
        copy.wait()


def pack(name, out_shapes, sources, plan):
    count = len(plan(0))

    def kernel(*refs):
        source_refs, outs, sems = refs[: len(sources)], refs[len(sources) : -1], refs[-1]
        pairs = []
        for i, at, width, o, row, column in plan(lax.axis_index("seq")):
            rows = source_refs[i].shape[0]
            if not isinstance(at, int):
                at = pl.multiple_of(at, DH)
            pairs.append(
                (
                    source_refs[i].at[:, pl.ds(at, width)],
                    outs[o].at[row : row + rows, column : column + width],
                )
            )
        copy_all(pairs, sems)

    return list(
        pl.pallas_call(
            kernel,
            out_shape=out_shapes,
            in_specs=[in_hbm()] * len(sources),
            out_specs=[anywhere()] * len(out_shapes),
            scratch_shapes=[pltpu.SemaphoreType.DMA((count,))],
            compiler_params=limit(1),
            cost_estimate=cost(0, 4 * sum(math.prod(o.shape) for o in out_shapes)),
            name=name,
        )(*[pltpu.with_memory_space_constraint(x, pltpu.HBM) for x in sources])
    )


def pack_pieces(groups, members, lists, sources, name):
    rows, columns = sources[0].shape
    width = columns // groups

    def plan(seq):
        return [
            (i, lax.rem(seq // members + r, groups) * width + h * DH, DH, n * groups + r, 0, j * DH)
            for n, blocks in enumerate(lists)
            for j, (i, h) in enumerate(blocks)
            for r in range(groups)
        ]

    outs = pack(
        name,
        [shape(rows, DH * len(blocks)) for blocks in lists for _ in range(groups)],
        sources,
        plan,
    )
    return [outs[n * groups : (n + 1) * groups] for n in range(len(lists))]


def pack_cross(bit, go, q, k, v):
    rows, columns = q.shape
    half = columns // 2
    more = k.shape[0]

    def plan(seq):
        xi = lax.rem(seq // bit, 2)
        at = ((1 - xi) if go else xi) * half
        return [
            (0, at, half, 0, 0, 0),
            (1, at, half, 0, rows, 0),
            (2, at, half, 0, rows + more, 0),
        ]

    name = "pack_go" if go else "pack_stay"
    return pack(name, [shape(rows + 2 * more, half)], [q, k, v], plan)[0]


def attend(queries, first, pairs, earlier, chosen, factor):
    parts = len(queries)
    rows = queries[0].shape[0]
    before = earlier[0].shape[1] if earlier else 0
    total_keys = sum(p.shape[0] for p in pairs)
    heads = len(chosen)

    def kernel(*refs):
        query_refs, refs = refs[:parts], refs[parts:]
        pair_refs, refs = refs[: len(pairs)], refs[len(pairs) :]
        early, outs = refs[:-parts], refs[-parts:]
        if before:
            for i in range(parts):
                outs[i][:, :before] = early[i][...]
        for j, h in enumerate(chosen):
            keys = [ref[:, 2 * j * DH : (2 * j + 1) * DH] for ref in pair_refs]
            values = [ref[:, (2 * j + 1) * DH : (2 * j + 2) * DH] for ref in pair_refs]
            at = first + h * DH
            for i in range(parts):
                outs[i][:, before + j * DH : before + (j + 1) * DH] = softmax_mix(
                    query_refs[i][:, at : at + DH], keys, values, factor
                ).astype(BF16)

    return pl.pallas_call(
        kernel,
        out_shape=[shape(rows, before + heads * DH)] * parts,
        in_specs=[in_vmem()] * (parts + len(pairs) + len(earlier)),
        out_specs=[in_vmem()] * parts,
        compiler_params=limit(14),
        cost_estimate=cost(
            4 * heads * parts * rows * total_keys * DH,
            heads * total_keys * DH * 4,
            heads * parts * rows * total_keys,
        ),
        name="attend_%d" % chosen[0],
    )(*queries, *pairs, *earlier)


def cross(queries, captions, rows, block, factor):
    parts = len(queries)
    columns = queries[0].shape[1]
    total_keys = sum(c.shape[0] for c in captions) // 2

    def kernel(*refs):
        query_refs, caption_refs, outs = refs[:parts], refs[parts:-parts], refs[-parts:]
        for h in range(columns // DH):
            at = slice(h * DH, (h + 1) * DH)
            keys, values = [
                jnp.concatenate(
                    [
                        c[b * block : (b + 1) * block, at]
                        for c in caption_refs
                        for b in range(first, c.shape[0] // block, 2)
                    ],
                    axis=0,
                )
                for first in (0, 1)
            ]
            for query, out in zip(query_refs, outs):
                out[:, at] = softmax_mix(query[:rows, at], [keys], [values], factor).astype(
                    BF16
                )

    return pl.pallas_call(
        kernel,
        out_shape=[shape(rows, columns)] * parts,
        in_specs=[in_vmem()] * (parts + len(captions)),
        out_specs=[in_vmem()] * parts,
        compiler_params=limit(14),
        cost_estimate=cost(
            4 * parts * rows * total_keys * columns,
            (2 * parts * rows + 2 * total_keys) * columns * 2,
            parts * rows * total_keys * columns // DH,
        ),
        name="cross",
    )(*queries, *captions)


def project(members, tp_size, turn, lhs, weight, dtype, name):
    groups = len(lhs)
    rows, width = lhs[0].shape
    depth = weight.shape[0]
    columns = weight.shape[1] // tp_size

    def kernel(*refs):
        lhs_refs, w_ref, out = refs[:groups], refs[-2], refs[-1]
        zi = lax.axis_index("seq") // members
        side = lax.rem(lax.axis_index("tp") + turn, tp_size) if tp_size > 1 else 0
        block = math.gcd(columns, 512)
        for n in range(columns // block):
            at = pl.ds(pl.multiple_of(side * columns + n * block, DH), block)
            total = None
            for r in range(groups):
                base = pl.multiple_of(lax.rem(zi + r, groups) * width, DH)
                term = jnp.dot(
                    lhs_refs[r][...], w_ref[pl.ds(base, width), at], preferred_element_type=F32
                )
                total = term if total is None else total + term
            out[:, n * block : (n + 1) * block] = total.astype(out.dtype)

    return pl.pallas_call(
        kernel,
        out_shape=shape(rows, columns, dtype),
        in_specs=[in_vmem()] * (groups + 1),
        out_specs=in_vmem(),
        compiler_params=limit(24),
        cost_estimate=cost(
            2 * rows * depth * columns, depth * columns * 2 + rows * columns * 4
        ),
        name=name,
    )(*lhs, weight)


def finish(bit, tokens, gate, home, away, stay, came):
    def kernel(tokens, gate, home, away, stay, came, updated, cross_heads):
        projected = home[...] + away[...].astype(F32)
        updated[...] = (tokens[...].astype(F32) + gate[...] * projected).astype(BF16)
        half = stay.shape[1]
        xi = lax.rem(lax.axis_index("seq") // bit, 2)
        for side, half_heads in ((xi, stay), (1 - xi, came)):
            cross_heads[:, pl.ds(pl.multiple_of(side * half, DH), half)] = half_heads[...]

    return pl.pallas_call(
        kernel,
        out_shape=[shape(*tokens.shape), shape(stay.shape[0], 2 * stay.shape[1])],
        in_specs=[in_vmem()] * 6,
        out_specs=[in_vmem()] * 2,
        compiler_params=limit(12),
        cost_estimate=cost(0, tokens.size * 10),
        name="finish",
    )(tokens, gate[None, :], home, away, stay, came)


def shards(
    seq_size,
    tp_size,
    tokens,
    self_queries,
    self_keys,
    self_values,
    cross_queries,
    caption_keys,
    caption_values,
    out_weight,
    gate_vector,
):
    rows, columns = self_queries.shape
    heads_here = columns // DH
    factor = LOG2E / math.sqrt(DH)
    groups = math.gcd(heads_here, seq_size)
    members = seq_size // groups
    heads = heads_here // groups
    bit = members // 2
    cap_rows = caption_keys.shape[0]

    def rotate(x, r):
        if r % groups == 0:
            return x
        step = (r % groups) * members
        return lax.ppermute(x, "seq", [(s, (s + step) % seq_size) for s in range(seq_size)])

    def swap(x, by):
        return lax.ppermute(x, "seq", [(s, s ^ by) for s in range(seq_size)])

    def join(*xs):
        return xs[0] if len(xs) == 1 else jnp.concatenate(xs, axis=0)

    sources = [self_keys, self_values, self_queries]
    if (groups, members, tp_size) != (4, 4, 2):
        index_groups = [[g * members + m for m in range(members)] for g in range(groups)]

        def gather(x):
            return lax.all_gather(
                x, "seq", axis=0, tiled=True, axis_index_groups=index_groups
            )

        outs = []
        for h in range(heads):
            blocks = [(0, h), (1, h), (2, h)]
            (pieces,) = pack_pieces(groups, members, [blocks], sources, "pack_%d" % h)
            pieces = [rotate(x, r) for r, x in enumerate(pieces)]
            pair = gather(join(*[x[:, : 2 * DH] for x in pieces]))
            outs = attend(pieces, (2 - h) * DH, [pair], outs, [h], factor)
        lhs = [rotate(x, groups - r) for r, x in enumerate(outs)]
        caption = join(caption_keys, caption_values)
        caption = gather(join(*[rotate(caption, r) for r in range(groups)]))
        (cross_heads,) = cross([cross_queries], [caption], rows, cap_rows, factor)
        both = project(members, 1, 0, lhs, out_weight, BF16, "both")
        projected = lax.psum_scatter(both, "tp", scatter_dimension=1, tiled=True).astype(F32)
        updated = (tokens.astype(F32) + gate_vector[None, :] * projected).astype(BF16)
        return (updated, cross_heads)

    chunks = [list(range(2)), list(range(2, heads))]
    kv = [[(i, h) for h in chunk for i in range(2)] for chunk in chunks]
    kv[1] += [(2, h) for h in range(heads)]
    first = pack_pieces(groups, members, kv[:1], sources, "pack_first")[0]
    go = pack_cross(bit, True, cross_queries, caption_keys, caption_values)
    (second,) = pack_pieces(groups, members, kv[1:], sources, "pack_later")
    stay = pack_cross(bit, False, cross_queries, caption_keys, caption_values)

    def travel(pieces, gates):
        return pieces[:1] + [
            rotate(x if g is None else after(x, g), r + 1)
            for r, (x, g) in enumerate(zip(pieces[1:], gates))
        ]

    come = swap(go, bit)
    first = travel(first, [None] * 3)
    second = travel(second, [come, (first[1], come), (first[1], come)])
    mine = join(*first)
    half_first = join(mine, swap(mine, 2))
    caption = join(stay[rows:], come[rows:])
    pair = join(caption, swap(after(caption, first[1:]), members))
    at = 2 * DH * len(chunks[1])
    mine = join(*[x[:, :at] for x in second])
    half_second = join(mine, swap(after(mine, pair), 2))
    pairs_first = [half_first, swap(half_first, 1)]
    outs = attend(second, at, pairs_first, [], chunks[0], factor)
    beyond = swap(after(caption, pair), 2 * members)
    pairs_second = [half_second, swap(after(half_second, (outs, beyond)), 1)]
    outs = attend(second, at, pairs_second, outs, chunks[1], factor)
    last = swap(after(beyond, pair), members)
    other = join(beyond, last)
    lhs = [rotate(x, groups - r) for r, x in enumerate(outs)]

    away = project(members, tp_size, 1, lhs, out_weight, BF16, "away")
    captions = [after(pair, away), swap(after(pair, away), 1), other, swap(other, 1)]
    own, theirs = cross([stay, come], captions, rows, cap_rows, factor)
    came = swap(theirs, bit)
    away = lax.ppermute(away, "tp", [(0, 1), (1, 0)])
    home = project(members, tp_size, 0, lhs, out_weight, F32, "home")
    return tuple(finish(bit, tokens, gate_vector, home, away, own, came))


def solution(mesh):
    seq_size, tp_size = mesh.shape["seq"], mesh.shape["tp"]
    return jax.shard_map(
        lambda *args: shards(seq_size, tp_size, *args),
        mesh=mesh,
        in_specs=(
            P("seq", "tp"),
            P("seq", "tp"),
            P("seq", "tp"),
            P("seq", "tp"),
            P("seq", "tp"),
            P("seq", "tp"),
            P("seq", "tp"),
            P("tp", None),
            P("tp"),
        ),
        out_specs=(P("seq", "tp"), P("seq", "tp")),
        check_vma=False,
    )
```

```python
import math

import jax
import jax.numpy as jnp
from jax import lax
from jax.experimental import pallas as pl
from jax.experimental.pallas import tpu as pltpu
from jax.sharding import PartitionSpec as P

DH = 128
F32 = jnp.float32
BF16 = jnp.bfloat16
LOG2E = 1.4426950408889634


def in_vmem():
    return pl.BlockSpec(memory_space=pltpu.VMEM)


def anywhere():
    return pl.BlockSpec(memory_space=pl.ANY)


def in_hbm():
    return pl.BlockSpec(memory_space=pltpu.HBM)


def limit(mebibytes):
    return pltpu.CompilerParams(vmem_limit_bytes=mebibytes * 2**20)


def cost(flops, nbytes, transcendentals=0):
    return pl.CostEstimate(
        flops=int(flops), bytes_accessed=int(nbytes), transcendentals=int(transcendentals)
    )


def shape(rows, columns, dtype=BF16):
    return jax.ShapeDtypeStruct((rows, columns), dtype)


def after(x, *others):
    return lax.optimization_barrier((x, others))[0]


def softmax_mix(query, keys, values, factor):
    scores = [
        lax.dot_general(query, block, (((1,), (1,)), ((), ())), preferred_element_type=F32)
        for block in keys
    ]
    top = jnp.max(scores[0], axis=1, keepdims=True)
    for block in scores[1:]:
        top = jnp.maximum(top, jnp.max(block, axis=1, keepdims=True))
    mixed = None
    for block, value in zip(scores, values):
        weight = jnp.exp2((block - top) * factor).astype(BF16)
        wide = jnp.concatenate([value, jnp.ones_like(value)], axis=1)
        term = jnp.dot(weight, wide, preferred_element_type=F32)
        mixed = term if mixed is None else mixed + term
    return mixed[:, :DH] / mixed[:, DH:]


def copy_all(pairs, sems):
    copies = [
        pltpu.make_async_copy(source, target, sems.at[i])
        for i, (source, target) in enumerate(pairs)
    ]
    for copy in copies:
        copy.start()
    for copy in copies:
        copy.wait()


def pack(name, out_shapes, sources, plan):
    count = len(plan(0))

    def kernel(*refs):
        source_refs, outs, sems = refs[: len(sources)], refs[len(sources) : -1], refs[-1]
        pairs = []
        for i, at, width, o, row, column in plan(lax.axis_index("seq")):
            rows = source_refs[i].shape[0]
            if not isinstance(at, int):
                at = pl.multiple_of(at, DH)
            pairs.append(
                (
                    source_refs[i].at[:, pl.ds(at, width)],
                    outs[o].at[row : row + rows, column : column + width],
                )
            )
        copy_all(pairs, sems)

    return list(
        pl.pallas_call(
            kernel,
            out_shape=out_shapes,
            in_specs=[in_hbm()] * len(sources),
            out_specs=[anywhere()] * len(out_shapes),
            scratch_shapes=[pltpu.SemaphoreType.DMA((count,))],
            compiler_params=limit(1),
            cost_estimate=cost(0, 4 * sum(math.prod(o.shape) for o in out_shapes)),
            name=name,
        )(*[pltpu.with_memory_space_constraint(x, pltpu.HBM) for x in sources])
    )


def pack_pieces(groups, members, lists, sources, name):
    rows, columns = sources[0].shape
    width = columns // groups

    def plan(seq):
        return [
            (i, lax.rem(seq // members + r, groups) * width + h * DH, DH, n * groups + r, 0, j * DH)
            for n, blocks in enumerate(lists)
            for j, (i, h) in enumerate(blocks)
            for r in range(groups)
        ]

    outs = pack(
        name,
        [shape(rows, DH * len(blocks)) for blocks in lists for _ in range(groups)],
        sources,
        plan,
    )
    return [outs[n * groups : (n + 1) * groups] for n in range(len(lists))]


def pack_cross(bit, go, q, k, v):
    rows, columns = q.shape
    half = columns // 2
    more = k.shape[0]

    def plan(seq):
        xi = lax.rem(seq // bit, 2)
        at = ((1 - xi) if go else xi) * half
        return [
            (0, at, half, 0, 0, 0),
            (1, at, half, 0, rows, 0),
            (2, at, half, 0, rows + more, 0),
        ]

    name = "pack_go" if go else "pack_stay"
    return pack(name, [shape(rows + 2 * more, half)], [q, k, v], plan)[0]


def attend(queries, first, pairs, earlier, chosen, factor):
    parts = len(queries)
    rows = queries[0].shape[0]
    before = earlier[0].shape[1] if earlier else 0
    total_keys = sum(p.shape[0] for p in pairs)
    heads = len(chosen)

    def kernel(*refs):
        query_refs, refs = refs[:parts], refs[parts:]
        pair_refs, refs = refs[: len(pairs)], refs[len(pairs) :]
        early, outs = refs[:-parts], refs[-parts:]
        if before:
            for i in range(parts):
                outs[i][:, :before] = early[i][...]
        for j, h in enumerate(chosen):
            keys = [ref[:, 2 * j * DH : (2 * j + 1) * DH] for ref in pair_refs]
            values = [ref[:, (2 * j + 1) * DH : (2 * j + 2) * DH] for ref in pair_refs]
            at = first + h * DH
            for i in range(parts):
                outs[i][:, before + j * DH : before + (j + 1) * DH] = softmax_mix(
                    query_refs[i][:, at : at + DH], keys, values, factor
                ).astype(BF16)

    return pl.pallas_call(
        kernel,
        out_shape=[shape(rows, before + heads * DH)] * parts,
        in_specs=[in_vmem()] * (parts + len(pairs) + len(earlier)),
        out_specs=[in_vmem()] * parts,
        compiler_params=limit(14),
        cost_estimate=cost(
            4 * heads * parts * rows * total_keys * DH,
            heads * total_keys * DH * 4,
            heads * parts * rows * total_keys,
        ),
        name="attend_%d" % chosen[0],
    )(*queries, *pairs, *earlier)


def cross(queries, captions, rows, block, factor):
    parts = len(queries)
    columns = queries[0].shape[1]
    total_keys = sum(c.shape[0] for c in captions) // 2

    def kernel(*refs):
        query_refs, caption_refs, outs = refs[:parts], refs[parts:-parts], refs[-parts:]
        for h in range(columns // DH):
            at = slice(h * DH, (h + 1) * DH)
            keys, values = [
                jnp.concatenate(
                    [
                        c[b * block : (b + 1) * block, at]
                        for c in caption_refs
                        for b in range(first, c.shape[0] // block, 2)
                    ],
                    axis=0,
                )
                for first in (0, 1)
            ]
            for query, out in zip(query_refs, outs):
                out[:, at] = softmax_mix(query[:rows, at], [keys], [values], factor).astype(
                    BF16
                )

    return pl.pallas_call(
        kernel,
        out_shape=[shape(rows, columns)] * parts,
        in_specs=[in_vmem()] * (parts + len(captions)),
        out_specs=[in_vmem()] * parts,
        compiler_params=limit(14),
        cost_estimate=cost(
            4 * parts * rows * total_keys * columns,
            (2 * parts * rows + 2 * total_keys) * columns * 2,
            parts * rows * total_keys * columns // DH,
        ),
        name="cross",
    )(*queries, *captions)


def project(members, tp_size, turn, lhs, weight, dtype, name):
    groups = len(lhs)
    rows, width = lhs[0].shape
    depth = weight.shape[0]
    columns = weight.shape[1] // tp_size

    def kernel(*refs):
        lhs_refs, w_ref, out = refs[:groups], refs[-2], refs[-1]
        zi = lax.axis_index("seq") // members
        side = lax.rem(lax.axis_index("tp") + turn, tp_size) if tp_size > 1 else 0
        block = math.gcd(columns, 512)
        for n in range(columns // block):
            at = pl.ds(pl.multiple_of(side * columns + n * block, DH), block)
            total = None
            for r in range(groups):
                base = pl.multiple_of(lax.rem(zi + r, groups) * width, DH)
                term = jnp.dot(
                    lhs_refs[r][...], w_ref[pl.ds(base, width), at], preferred_element_type=F32
                )
                total = term if total is None else total + term
            out[:, n * block : (n + 1) * block] = total.astype(out.dtype)

    return pl.pallas_call(
        kernel,
        out_shape=shape(rows, columns, dtype),
        in_specs=[in_vmem()] * (groups + 1),
        out_specs=in_vmem(),
        compiler_params=limit(24),
        cost_estimate=cost(
            2 * rows * depth * columns, depth * columns * 2 + rows * columns * 4
        ),
        name=name,
    )(*lhs, weight)


def assemble(bit, stay, came):
    half = stay.shape[1]

    def kernel(stay_ref, came_ref, out):
        xi = lax.rem(lax.axis_index("seq") // bit, 2)
        for side, heads in ((xi, stay_ref), (1 - xi, came_ref)):
            out[:, pl.ds(pl.multiple_of(side * half, DH), half)] = heads[...]

    return pl.pallas_call(
        kernel,
        out_shape=shape(stay.shape[0], 2 * half),
        in_specs=[in_vmem()] * 2,
        out_specs=in_vmem(),
        compiler_params=limit(4),
        cost_estimate=cost(0, stay.size * 8),
        name="assemble",
    )(stay, came)


def finish(tokens, gate, home, away):
    def kernel(tokens, gate, home, away, updated):
        projected = home[...] + away[...].astype(F32)
        updated[...] = (tokens[...].astype(F32) + gate[...] * projected).astype(BF16)

    return pl.pallas_call(
        kernel,
        out_shape=shape(*tokens.shape),
        in_specs=[in_vmem()] * 4,
        out_specs=in_vmem(),
        compiler_params=limit(12),
        cost_estimate=cost(0, tokens.size * 10),
        name="finish",
    )(tokens, gate[None, :], home, away)


def shards(
    seq_size,
    tp_size,
    tokens,
    self_queries,
    self_keys,
    self_values,
    cross_queries,
    caption_keys,
    caption_values,
    out_weight,
    gate_vector,
):
    rows, columns = self_queries.shape
    heads_here = columns // DH
    factor = LOG2E / math.sqrt(DH)
    groups = math.gcd(heads_here, seq_size)
    members = seq_size // groups
    heads = heads_here // groups
    bit = members // 2
    cap_rows = caption_keys.shape[0]

    def rotate(x, r):
        if r % groups == 0:
            return x
        step = (r % groups) * members
        return lax.ppermute(x, "seq", [(s, (s + step) % seq_size) for s in range(seq_size)])

    def swap(x, by):
        return lax.ppermute(x, "seq", [(s, s ^ by) for s in range(seq_size)])

    def join(*xs):
        return xs[0] if len(xs) == 1 else jnp.concatenate(xs, axis=0)

    sources = [self_keys, self_values, self_queries]
    if (groups, members, tp_size) != (4, 4, 2):
        index_groups = [[g * members + m for m in range(members)] for g in range(groups)]

        def gather(x):
            return lax.all_gather(
                x, "seq", axis=0, tiled=True, axis_index_groups=index_groups
            )

        outs = []
        for h in range(heads):
            blocks = [(0, h), (1, h), (2, h)]
            (pieces,) = pack_pieces(groups, members, [blocks], sources, "pack_%d" % h)
            pieces = [rotate(x, r) for r, x in enumerate(pieces)]
            pair = gather(join(*[x[:, : 2 * DH] for x in pieces]))
            outs = attend(pieces, (2 - h) * DH, [pair], outs, [h], factor)
        lhs = [rotate(x, groups - r) for r, x in enumerate(outs)]
        caption = join(caption_keys, caption_values)
        caption = gather(join(*[rotate(caption, r) for r in range(groups)]))
        (cross_heads,) = cross([cross_queries], [caption], rows, cap_rows, factor)
        both = project(members, 1, 0, lhs, out_weight, BF16, "both")
        projected = lax.psum_scatter(both, "tp", scatter_dimension=1, tiled=True).astype(F32)
        updated = (tokens.astype(F32) + gate_vector[None, :] * projected).astype(BF16)
        return (updated, cross_heads)

    chunks = [list(range(2)), list(range(2, heads))]
    kv = [[(i, h) for h in chunk for i in range(2)] for chunk in chunks]
    kv[1] += [(2, h) for h in range(heads)]
    first = pack_pieces(groups, members, kv[:1], sources, "pack_first")[0]
    go = pack_cross(bit, True, cross_queries, caption_keys, caption_values)
    (second,) = pack_pieces(groups, members, kv[1:], sources, "pack_later")
    stay = pack_cross(bit, False, cross_queries, caption_keys, caption_values)

    def travel(pieces, gates):
        return pieces[:1] + [
            rotate(x if g is None else after(x, g), r + 1)
            for r, (x, g) in enumerate(zip(pieces[1:], gates))
        ]

    come = swap(go, bit)
    first = travel(first, [None] * 3)
    second = travel(second, [come, (first[1], come), (first[1], come)])
    mine = join(*first)
    half_first = join(mine, swap(mine, 2))
    caption = join(stay[rows:], come[rows:])
    pair = join(caption, swap(after(caption, first[1:]), members))
    at = 2 * DH * len(chunks[1])
    mine = join(*[x[:, :at] for x in second])
    half_second = join(mine, swap(after(mine, pair), 2))
    pairs_first = [half_first, swap(half_first, 1)]
    outs = attend(second, at, pairs_first, [], chunks[0], factor)
    beyond = swap(after(caption, pair), 2 * members)
    pairs_second = [half_second, swap(after(half_second, (outs, beyond)), 1)]
    outs = attend(second, at, pairs_second, outs, chunks[1], factor)
    last = swap(after(beyond, pair), members)
    other = join(beyond, last)
    lhs = [rotate(x, groups - r) for r, x in enumerate(outs)]

    away = project(members, tp_size, 1, lhs, out_weight, BF16, "away")
    captions = [after(pair, away), swap(after(pair, away), 1), other, swap(other, 1)]
    own, theirs = cross([stay, come], captions, rows, cap_rows, factor)
    came = swap(theirs, bit)
    away = lax.ppermute(away, "tp", [(0, 1), (1, 0)])
    home = project(members, tp_size, 0, lhs, out_weight, F32, "home")
    cross_heads = assemble(bit, own, came)
    return (finish(tokens, gate_vector, home, away), cross_heads)


def solution(mesh):
    seq_size, tp_size = mesh.shape["seq"], mesh.shape["tp"]
    return jax.shard_map(
        lambda *args: shards(seq_size, tp_size, *args),
        mesh=mesh,
        in_specs=(
            P("seq", "tp"),
            P("seq", "tp"),
            P("seq", "tp"),
            P("seq", "tp"),
            P("seq", "tp"),
            P("seq", "tp"),
            P("seq", "tp"),
            P("tp", None),
            P("tp"),
        ),
        out_specs=(P("seq", "tp"), P("seq", "tp")),
        check_vma=False,
    )
```
